256 devices in a mesh: gx: 8 (over y_hi, x), gy: 8 (over z), scene: 4 (over y_lo, core).
Axes of the slice: x: 4, y: 4 (y_hi: 2, y_lo: 2; y = y_hi * 2 + y_lo), z: 8, core: 2. Of those that a mesh axis runs over, the one named last changes fastest.
Arguments:
- field_in: bfloat16 [4, 32, 128, 128, 256], P('scene', None, 'gx', 'gy'), may hold values from -6 to 6
- grad_pre: bfloat16 [4, 32, 128, 128, 256], P('scene', None, 'gx', 'gy'), may hold values from -6 to 6
- spec_weight: bfloat16 [24, 24, 13, 2, 1024], P('gx', 'gy'), may hold values from -6 to 6
- point_weight: bfloat16 [32, 32], replicated, may hold values from -1 to 1
Outputs:
- grad_field: bfloat16 [4, 32, 128, 128, 256], P('scene', None, 'gx', 'gy')
- grad_spec: float32 [24, 24, 13, 2, 1024], P('gx', 'gy', None, None, 'scene')
The draws below stay inside these ranges and needn't reach their ends.
All inputs are finite; a program needn't handle non-finite values.
Results may differ from the reference program's by a relative error of at most 0.0045.
Values may be sent and summed in bfloat16 or wider, within the bound.
A program may use at most 128 MiB of HBM per device.

```python
import math
import jax
import jax.numpy as jnp
from jax import lax

C = 32
MX = 24
MY = 24
MZ = 13
NZ = 256
SCENES = 4
NX = 128
NY = 128


def block_scale(own_key, dims, cuts, least, largest):
    def one(dim, parts):
        steps = jax.random.uniform(jax.random.fold_in(jax.random.fold_in(own_key, 6), dim), (parts,), jnp.float32, least / len(cuts), largest / len(cuts))
        return jnp.repeat(jnp.exp(steps), dims[dim] // parts).reshape((-1,) + (1,) * (len(dims) - dim - 1))

    level = one(*cuts[0])
    for cut in cuts[1:]:
        level = level * one(*cut)
    return level


def normal_values(own_key, extent, spread, most, pieces=(), kind=jnp.bfloat16):
    result = spread * jax.random.normal(own_key, extent, jnp.float32)
    if pieces:
        result = result * block_scale(own_key, extent, pieces, -0.22, 0.18)
    return jnp.clip(result, -most, most).astype(kind)


def setup_inputs(seed: int = 0) -> dict:
    seeds = jax.random.split(jax.random.key(seed), 5)
    field_in = normal_values(seeds[0], (SCENES, C, NX, NY, NZ), 1.0, 6.0, ((0, 4), (2, 8), (3, 8)))
    grad_pre = normal_values(seeds[1], (SCENES, C, NX, NY, NZ), 1.0, 6.0, ((0, 4), (2, 8), (3, 8)))
    spec_weight = normal_values(seeds[2], (MX, MY, MZ, 2, C * C), ((NX * NY * NZ / (4 * MX * MY * MZ * C)) ** 0.5), 6.0, ((0, 8), (1, 8)))
    point_weight = normal_values(seeds[3], (C, C), C ** -0.5, 1.0)
    return {"field_in": field_in, "grad_pre": grad_pre, "spec_weight": spec_weight, "point_weight": point_weight}


def angle_table(index, modes, positions, length):
    signed_freq = jnp.where(index < modes // 2, index, index - modes)
    turns = jnp.mod(signed_freq[..., None] * positions, length)
    return turns.astype(jnp.float32) * (2.0 * math.pi / length)


def forward_rotation(angles):
    cosine = jnp.cos(angles)
    sine = jnp.sin(angles)
    return jnp.stack([jnp.stack([cosine, sine], -1), jnp.stack([-sine, cosine], -1)], 0)


def inverse_rotation(angles):
    cosine = jnp.cos(angles)
    sine = jnp.sin(angles)
    return jnp.stack([jnp.stack([cosine, -sine], -1), jnp.stack([sine, cosine], -1)], 0)


def z_tables(modes_z, length):
    angles = angle_table(jnp.arange(modes_z, dtype=jnp.int32), 2 * modes_z, jnp.arange(length, dtype=jnp.int32), length)
    cosine = jnp.cos(angles)
    sine = jnp.sin(angles)
    forward_z = jnp.concatenate([cosine, -sine], 0).T.astype(jnp.bfloat16)
    inverse_z = jnp.stack([cosine, -sine], 0)
    return forward_z, inverse_z


def reference(field_in, grad_pre, spec_weight, point_weight):
    highest = lax.Precision.HIGHEST
    norm = float(NX * NY * NZ) ** -0.5
    forward_z, inverse_z = z_tables(MZ, NZ)
    angles_y = angle_table(jnp.arange(MY, dtype=jnp.int32), MY, jnp.arange(NY, dtype=jnp.int32), NY)
    angles_x = angle_table(jnp.arange(MX, dtype=jnp.int32), MX, jnp.arange(NX, dtype=jnp.int32), NX)
    forward_y = forward_rotation(angles_y)
    forward_x = forward_rotation(angles_x)
    inverse_y = inverse_rotation(angles_y)
    inverse_x = inverse_rotation(angles_x)
    z_weight = jnp.where(jnp.arange(MZ, dtype=jnp.int32) == 0, 1.0, 2.0).astype(jnp.float32)
    weights = spec_weight.astype(jnp.float32).reshape(MX, MY, MZ, 2, C, C)
    weight_re = weights[:, :, :, 0]
    weight_im = weights[:, :, :, 1]
    mixing = point_weight.astype(jnp.float32)
    grad_total = jnp.zeros((MX, MY, MZ, 2, C, C), jnp.float32)
    results = []
    for scene_index in range(SCENES):
        field_z = jnp.dot(field_in[scene_index].reshape(-1, NZ), forward_z, preferred_element_type=jnp.float32).reshape(C, NX, NY, 2, MZ)
        pre_z = jnp.dot(grad_pre[scene_index].reshape(-1, NZ), forward_z, preferred_element_type=jnp.float32).reshape(C, NX, NY, 2, MZ)
        along_z = jnp.stack([field_z, pre_z], 0)
        along_y = jnp.einsum('wcxypk,qjyp->wcxqjk', along_z, forward_y, precision=highest)
        spectra = jnp.einsum('wcxqjk,rixq->ijwcrk', along_y, forward_x, precision=highest) * norm
        field_hat = spectra[:, :, 0]
        grad_out = spectra[:, :, 1] * z_weight
        hat_re = field_hat[:, :, :, 0]
        hat_im = field_hat[:, :, :, 1]
        out_re = grad_out[:, :, :, 0]
        out_im = grad_out[:, :, :, 1]
        mode_re = jnp.einsum('abkio,abok->abik', weight_re, out_re, precision=highest) + jnp.einsum('abkio,abok->abik', weight_im, out_im, precision=highest)
        mode_im = jnp.einsum('abkio,abok->abik', weight_re, out_im, precision=highest) - jnp.einsum('abkio,abok->abik', weight_im, out_re, precision=highest)
        mode_grad = jnp.stack([mode_re, mode_im], 3)
        rounded = lax.optimization_barrier(mode_grad.astype(jnp.bfloat16)).astype(jnp.float32)
        grad_re = jnp.einsum('abok,abik->abkio', out_re, hat_re, precision=highest) + jnp.einsum('abok,abik->abkio', out_im, hat_im, precision=highest)
        grad_im = jnp.einsum('abok,abik->abkio', out_im, hat_re, precision=highest) - jnp.einsum('abok,abik->abkio', out_re, hat_im, precision=highest)
        grad_total = grad_total + jnp.stack([grad_re, grad_im], 3)
        back_y = jnp.einsum('ijcpk,qjyp->iycqk', rounded, inverse_y, precision=highest)
        back_modes = jnp.einsum('iycqk,rixq->xycrk', back_y, inverse_x, precision=highest)
        spectral_grad = jnp.einsum('xycrk,rkz->cxyz', back_modes, inverse_z, precision=highest) * norm
        local_grad = jnp.einsum('oi,oxyz->ixyz', mixing, grad_pre[scene_index].astype(jnp.float32))
        results.append((spectral_grad + local_grad).astype(jnp.bfloat16))
    return jnp.stack(results, 0), grad_total.reshape(MX, MY, MZ, 2, C * C)
```

```python
import functools

import jax
import jax.numpy as jnp
import numpy as np
from jax import lax
from jax.experimental import pallas as pl
from jax.experimental.pallas import tpu as pltpu
from jax.sharding import PartitionSpec as P

MZ = 13
NZ = 256
MESH = pl.DeviceIdType.MESH
F32 = jnp.float32
BF16 = jnp.bfloat16
NT_DIMS = (((1,), (1,)), ((), ()))
ROWS = 120


def split_np(value):
    hi = value.astype(np.float32).astype(jnp.bfloat16)
    lo = (value - hi.astype(np.float64)).astype(jnp.bfloat16)
    return hi, lo


def signed(j, m):
    return np.where(j < m // 2, j, j - m)


@functools.lru_cache
def tables(gx, gy):
    mx, my, nx, ny = 3 * gx, 3 * gy, 16 * gx, 16 * gy
    norm = float(nx * ny * NZ) ** -0.5
    out = {}
    k = np.arange(14)
    ang = 2 * np.pi * ((k[:, None] * np.arange(NZ)[None]) % NZ) / NZ
    keep = (k < MZ)[:, None]
    zt = np.stack([np.cos(ang) * keep, -np.sin(ang) * keep])
    out["texp"] = np.repeat(zt.reshape(28, NZ), 8, axis=0).astype(np.float32).astype(jnp.bfloat16)
    fx, fy = signed(np.arange(mx), mx), signed(np.arange(my), my)
    m = np.arange(9)
    a, b = m // 3, m % 3
    kx = fx[3 * np.arange(gx)[None, :] + a[:, None]]
    ky = fy[3 * np.arange(gy)[:, None] + b[None, :]]
    kx = np.broadcast_to(kx[None], (gy, 9, gx)).reshape(gy, -1)
    ky = np.broadcast_to(ky[:, :, None], (gy, 9, gx)).reshape(gy, -1)
    xl, yl = np.repeat(np.arange(16), 16), np.tile(np.arange(16), 16)
    ang = 2 * np.pi * (kx[..., None] * xl / nx + ky[..., None] * yl / ny)
    out["m0"] = np.concatenate([*split_np(np.cos(ang)), *split_np(np.sin(ang))], axis=1)
    ph = np.zeros((gy, 9 * gx, 128), np.float32)
    theta = 2 * np.pi * ((kx[..., None] * np.arange(gx)) % gx) / gx
    phi = 2 * np.pi * ((ky[..., None] * np.arange(gy)) % gy) / gy
    ph[..., 0:gx] = np.cos(theta)
    ph[..., 8 : 8 + gx] = np.sin(theta)
    ph[..., 16 : 16 + gy] = np.cos(phi)
    ph[..., 24 : 24 + gy] = np.sin(phi)
    out["ph"] = ph
    delta = np.array([[0, np.pi / 2], [-np.pi / 2, 0]])
    col_src = np.concatenate([np.repeat(np.arange(gy), 16), np.tile(np.arange(gy), 2)])
    col_p = np.concatenate([np.tile(np.repeat([0, 1], 8), gy), np.repeat([0, 1], gy)])
    col_m = np.concatenate([np.tile(np.arange(8), 2 * gy), np.full(2 * gy, 8)])
    row_p, row_a, row_y = np.repeat([0, 1], 48), np.tile(np.repeat([0, 1, 2], 16), 2), np.tile(np.arange(16), 6)
    col_ky = fy[3 * col_src + col_m % 3]
    ang = 2 * np.pi * col_ky[None] * row_y[:, None] / ny + delta[row_p[:, None], col_p[None]]
    match = row_a[:, None] == (col_m // 3)[None]
    out["ty"] = np.stack([np.cos(ang) * match, np.sin(ang) * match]).astype(np.float32)
    phi = 2 * np.pi * ((np.arange(gy)[:, None] * col_ky[None]) % gy) / gy
    out["phy"] = np.stack([np.cos(phi), np.sin(phi)]).astype(np.float32)
    col = np.arange(96 * gx)
    col_kx = fx[3 * (col // 96) + col // 16 % 3]
    col_p = col // 48 % 2
    row_p, row_x = np.repeat([0, 1], 16), np.tile(np.arange(16), 2)
    ang = 2 * np.pi * col_kx[None] * row_x[:, None] / nx + delta[row_p[:, None], col_p[None]]
    out["tx"] = np.stack([np.cos(ang), np.sin(ang)]).astype(np.float32)
    psi = 2 * np.pi * ((np.arange(gx)[:, None] * col_kx[None]) % gx) / gx
    out["phx"] = np.stack([np.cos(psi), np.sin(psi)]).astype(np.float32)
    rep = np.zeros((2, ROWS, 24))
    rs = np.zeros((2, 32, ROWS))
    mk1 = np.zeros((ROWS, 128))
    mk2 = np.zeros((ROWS, 128))
    for row in range(9 * MZ):
        mode, kz = divmod(row, MZ)
        mk1[row] = np.arange(128) // 8 == kz
        mk2[row] = np.arange(128) % 16 == kz
        for p in range(2):
            rep[p, row, p * 9 + mode] = 1
            rs[p, p * 8 + mode if mode < 8 else 16 + p, row] = 1
    out["rep"], out["rs"] = rep.astype(jnp.bfloat16), rs.astype(jnp.bfloat16)
    out["mk1"], out["mk2"] = mk1.astype(np.float32), mk2.astype(np.float32)
    k = np.arange(16)
    ang = 2 * np.pi * ((k[:, None] * np.arange(NZ)[None]) % NZ) / NZ
    keep = (k < MZ)[:, None] * norm
    zt = np.stack([np.cos(ang) * keep, -np.sin(ang) * keep])
    out["zb"] = zt.astype(np.float32).astype(jnp.bfloat16)
    return out


def split(value):
    hi = value.astype(BF16)
    return hi, (value - hi.astype(F32)).astype(BF16)


def dot(a, b):
    return jnp.dot(a, b, preferred_element_type=F32)


def dot_split(value, table):
    hi, lo = split(value)
    return dot(hi, table) + dot(lo, table)


def one_hot(cond, value=1.0):
    return jnp.where(cond, value, 0.0).astype(BF16)


def iota(shape, dim):
    return lax.broadcasted_iota(jnp.int32, shape, dim)


def far_offsets(n):
    half = n // 2
    order = []
    for t in range(n - 1):
        order.append(half + t // 2 if t % 2 == 0 else half - (t + 1) // 2)
    return order


def comm_kernel(
    gx, gy, ns, norm,
    xf_hbm, xp_hbm, w_hbm, pw_hbm, texp_hbm, m0_hbm, ph_hbm, ty_hbm, phy_hbm, tx_hbm, phx_hbm,
    rep_hbm, rs_hbm, mk1_hbm, mk2_hbm,
    b_out, loc_hbm, gs_out,
    xf, xp, w, pw, texp, m0, ph, ty, phy, tx, phx, rep, rs, mk1, mk2,
    tj, send1, recv1, acc_c, acc_s, send2, recv2, sum2, send3, recv3, tbuf,
    send_a, recv_a, send_b, recv_b, send_g, recv_g, tyh, tyl, txh, txl, kron, stage,
    sel, orep, selo, rc,
    load_f, load_p, load_c, loc_sem,
    s1s, s1r, s2s, s2r, s3s, s3r, sas, sar, sbs, sbr, sgs, sgr, sts, str_,
):
    c = 4 * gx
    cc = c * c
    me_x, me_y, me_s = lax.axis_index("gx"), lax.axis_index("gy"), lax.axis_index("scene")

    def peer_x(t):
        if gx == 8:
            e = jnp.where(t % 4 < 2, 2 + t % 4, 3 - t % 4)
            f = jnp.where(t < 4, 1, 0)
            return lax.rem(me_x // 4 + f, 2) * 4 + lax.rem(me_x % 4 + e, 4)
        return lax.rem(me_x + 1 + t, gx)

    def peer_y(t):
        return lax.rem(me_y + far_offsets(gy)[t], gy)

    def rcopy(src, dst, ssem, rsem, device):
        return pltpu.make_async_remote_copy(
            src_ref=src, dst_ref=dst, send_sem=ssem, recv_sem=rsem, device_id=device, device_id_type=MESH
        )

    loads = [
        pltpu.make_async_copy(s, d, load_c.at[i])
        for i, (s, d) in enumerate(
            [
                (texp_hbm, texp), (m0_hbm, m0), (ph_hbm, ph), (pw_hbm, pw), (tx_hbm, tx), (phx_hbm, phx),
                (ty_hbm, ty), (phy_hbm, phy), (rep_hbm, rep), (rs_hbm, rs), (mk1_hbm, mk1), (mk2_hbm, mk2),
                (w_hbm, w),
            ]
        )
    ]

    def chunk(hbm, vmem, sems, t):
        rows = pl.ds(peer_x(t) * 4, 4)
        return pltpu.make_async_copy(hbm.at[rows], vmem.at[rows], sems.at[t])

    loads[0].start()
    for t in range(gx):
        chunk(xf_hbm, xf, load_f, t).start()
        chunk(xp_hbm, xp, load_p, t).start()
    for copy in loads[1:]:
        copy.start()

    barrier = pltpu.get_barrier_semaphore()
    for t in range(gx - 1):
        pl.semaphore_signal(barrier, inc=1, device_id={"gx": peer_x(t)}, device_id_type=MESH)
    for t in range(gy - 1):
        pl.semaphore_signal(barrier, inc=1, device_id={"gy": peer_y(t)}, device_id_type=MESH)
    for t in range(1, ns):
        pl.semaphore_signal(
            barrier, inc=1, device_id={"scene": lax.rem(me_s + t, ns)}, device_id_type=MESH
        )

    loads[0].wait()
    row_j = iota((224, NZ), 0) & 7
    for j in range(8):
        tj[j] = jnp.where(row_j == j, texp[...].astype(F32), 0.0).astype(BF16)

    def z_modes(t):
        d = peer_x(t)
        chunk(xf_hbm, xf, load_f, t).wait()
        chunk(xp_hbm, xp, load_p, t).wait()
        total = None
        for j in range(8):
            plane = xf[d * 4 + j] if j < 4 else xp[d * 4 + j - 4]
            part = lax.dot_general(tj[j], plane, NT_DIMS, preferred_element_type=F32)
            total = part if total is None else total + part
        return total.astype(BF16).reshape(2, 112, NZ)

    pl.semaphore_wait(barrier, gx + gy + ns - 3)

    def send_planes(t):
        return rcopy(
            send1.at[t], recv1.at[me_x], s1s.at[t], s1r.at[me_x], {"gx": peer_x(t)}
        )

    @pl.loop(0, gx - 1)
    def _(t):
        send1[t] = z_modes(t)
        send_planes(t).start()

    recv1[me_x] = z_modes(gx - 1)

    for copy in loads[1:]:
        copy.wait()
    acc_c[...] = jnp.zeros_like(acc_c)
    acc_s[...] = jnp.zeros_like(acc_s)
    send3[...] = jnp.zeros_like(send3)
    cells = 16 * c
    spread = one_hot(iota((cells, c), 0) >> 4 == iota((cells, c), 1))
    pw_t = lax.dot_general(spread, pw[...], NT_DIMS, preferred_element_type=F32).astype(BF16)
    wide = lax.dot_general(pw_t, spread, NT_DIMS, preferred_element_type=F32)
    same = (iota((cells, cells), 0) & 15) == (iota((cells, cells), 1) & 15)
    kron[...] = jnp.where(same, wide, 0.0).astype(BF16)

    def put_local(g):
        rows = pl.ds(pl.multiple_of(g * 16, 16), 16)
        return pltpu.make_async_copy(stage.at[lax.rem(g, 2)], loc_hbm.at[:, rows, :], loc_sem.at[lax.rem(g, 2)])

    @pl.loop(0, 16)
    def _(g):
        @pl.when(g >= 2)
        def _():
            put_local(g - 2).wait()

        rows = pl.ds(pl.multiple_of(g * 16, 16), 16)
        tile = xp[:, rows, :].reshape(cells, NZ)
        mixed = dot(kron[...], tile)
        stage[lax.rem(g, 2)] = mixed.astype(BF16).reshape(c, 16, NZ)
        put_local(g).start()

    def sel_table(p):
        r, l = iota((gx * 128, 128), 0), iota((gx * 128, 128), 1)
        j, k = r & 7, (r >> 3) & 15
        lane = jnp.where(j < 4, (2 + p) * c, p * c) + 4 * (r >> 7) + (j & 3)
        value = jnp.where((j < 4) | (k == 0), norm, 2.0 * norm)
        return jnp.where(l == lane, value, 0.0).astype(BF16)

    bits = c.bit_length() - 1
    for p in range(2):
        sel[p] = sel_table(p)
        selo[p] = one_hot((iota((cc, 128), 0) >> bits) + p * c == iota((cc, 128), 1))
        orep[p] = one_hot((iota((128, cc), 1) & (c - 1)) + p * c == iota((128, cc), 0))
        rc[p] = one_hot((iota((128, cells), 1) >> 4) + p * c == iota((128, cells), 0))
    ty_now = ty[0] * phy[0, pl.ds(me_y, 1), :] - ty[1] * phy[1, pl.ds(me_y, 1), :]
    tyh[...], tyl[...] = split(ty_now)
    kx = 96 * gx
    y_match = (iota((16, kx), 0)) == (iota((16, kx), 1) & 15)
    tx_now = tx[0] * phx[0, pl.ds(me_x, 1), :] - tx[1] * phx[1, pl.ds(me_x, 1), :]
    for r in range(32):
        row = jnp.where(y_match, jnp.broadcast_to(tx_now[r : r + 1], (16, kx)), 0.0)
        txh[r * 16 : r * 16 + 16], txl[r * 16 : r * 16 + 16] = split(row)

    nb = 9 * gx
    lane = iota((nb, 128), 1)

    def column(table, index):
        return jnp.sum(jnp.where(lane == index, table, 0.0), axis=1, keepdims=True)

    def add_source(s):
        cos_t, sin_t = column(ph[0], s), column(ph[0], 8 + s)
        gap = jnp.zeros((16, NZ), BF16)
        block = jnp.concatenate([recv1[s, 0], gap, recv1[s, 1], gap], axis=0)

        @pl.loop(0, gy)
        def _(g):
            part = lax.dot_general(m0[g], block, NT_DIMS, preferred_element_type=F32)
            part_c = part[0:nb] + part[nb : 2 * nb]
            part_s = part[2 * nb : 3 * nb] + part[3 * nb : 4 * nb]
            acc_c[g] += cos_t * part_c - sin_t * part_s
            acc_s[g] += cos_t * part_s + sin_t * part_c

    add_source(me_x)

    @pl.loop(0, gx - 1)
    def _(i):
        t = gx - 2 - i
        s = peer_x(t)
        rcopy(send1.at[t], recv1.at[s], s1s.at[t], s1r.at[s], {"gx": s}).wait_recv()
        add_source(s)

    def modes_for(g):
        cos_t, sin_t = column(ph[g], 16 + me_y), column(ph[g], 24 + me_y)
        total_c, total_s = acc_c[g], acc_s[g]
        turned_c = cos_t * total_c - sin_t * total_s
        turned_s = cos_t * total_s + sin_t * total_c
        re = turned_c[:, :128] + turned_s[:, 128:]
        im = turned_c[:, 128:] - turned_s[:, :128]
        return jnp.concatenate([re, im], axis=0).astype(BF16)

    def send_modes(t):
        return rcopy(send2.at[t], recv2.at[me_y], s2s.at[t], s2r.at[me_y], {"gy": peer_y(t)})

    for t in range(gy - 1):
        send2[t] = modes_for(peer_y(t))
        send_modes(t).start()
    total = modes_for(me_y).astype(F32)
    for t in reversed(range(gy - 1)):
        s = peer_y(t)
        rcopy(send2.at[t], recv2.at[s], s2s.at[t], s2r.at[s], {"gy": s}).wait_recv()
        total = total + recv2[s].astype(F32)
    sum2[...] = total

    for g in range(gx):
        send3[g, 0:18, :] = sum2[pl.ds(g, 18, stride=gx), :]

    def send_block(t):
        d = peer_x(t)
        return rcopy(send3.at[d], recv3.at[me_x], s3s.at[t], s3r.at[me_x], {"gx": d})

    for t in range(gx - 1):
        send_block(t).start()
    recv3[me_x] = send3[me_x]
    for t in range(gx - 1):
        s = peer_x(t)
        rcopy(send3.at[s], recv3.at[s], s3s.at[t], s3r.at[s], {"gx": s}).wait_recv()

    spectra = jnp.concatenate([recv3[s] for s in range(gx)], axis=1)
    sp_hi, sp_lo = split(spectra)
    mask = jnp.concatenate([mk1[...]] * gx, axis=1)
    table = None
    for p in range(2):
        rows = (dot(rep[p], sp_hi) + dot(rep[p], sp_lo)) * mask
        part = dot_split(rows, sel[p])
        table = part if table is None else table + part
    tbuf[me_s] = table

    def send_table(t):
        return rcopy(
            tbuf.at[me_s], tbuf.at[me_s], sts.at[t], str_.at[me_s], {"scene": lax.rem(me_s + t, ns)}
        )

    for t in range(1, ns):
        send_table(t).start()

    o_re, o_im = dot_split(table, orep[0]), dot_split(table, orep[1])
    w_re, w_im = w[0].astype(F32), w[1].astype(F32)
    grad = dot_split(w_re * o_re + w_im * o_im, selo[0]) + dot_split(w_re * o_im - w_im * o_re, selo[1])
    grad = grad.astype(BF16)
    mask = jnp.concatenate([mk2[...]] * (cells // 128), axis=1)
    modes = None
    for p in range(2):
        part = dot(rs[p], (dot(grad, rc[p]) * mask).astype(BF16))
        modes = part if modes is None else modes + part
    tiles = cells // 128
    send_a[...] = modes[0:16].astype(BF16)
    for p in range(2):
        for t in range(tiles):
            send_b[p * tiles + t : p * tiles + t + 1, :] = modes[16 + p : 17 + p, t * 128 : t * 128 + 128]

    def send_mode_grads(t):
        d = {"gy": peer_y(t)}
        rows = pl.ds(pl.multiple_of(me_y * 8, 8), 8)
        return (
            rcopy(send_a, recv_a.at[me_y], sas.at[t], sar.at[me_y], d),
            rcopy(send_b, recv_b.at[rows], sbs.at[t], sbr.at[me_y], d),
        )

    for t in range(gy - 1):
        for copy in send_mode_grads(t):
            copy.start()
    recv_a[me_y] = send_a[...]
    recv_b[pl.ds(pl.multiple_of(me_y * 8, 8), 8), :] = send_b[...]
    for t in range(gy - 1):
        s = peer_y(t)
        rcopy(send_a, recv_a.at[s], sas.at[t], sar.at[s], {"gy": s}).wait_recv()
        rows = pl.ds(pl.multiple_of(s * 8, 8), 8)
        rcopy(send_b, recv_b.at[rows], sbs.at[t], sbr.at[s], {"gy": s}).wait_recv()

    main = recv_a[...].reshape(16 * gy, cells)
    last = jnp.concatenate(
        [
            jnp.concatenate([recv_b[pl.ds(p * tiles + t, gy, stride=8), :] for p in range(2)], axis=0)
            for t in range(tiles)
        ],
        axis=1,
    ).astype(BF16)
    ka = 16 * gy
    back = dot(tyh[:, :ka], main) + dot(tyl[:, :ka], main)
    back = back + dot(tyh[:, ka:], last) + dot(tyl[:, ka:], last)
    send_g[...] = back.astype(BF16)

    def send_back(t):
        return rcopy(send_g, recv_g.at[me_x], sgs.at[t], sgr.at[me_x], {"gx": peer_x(t)})

    for t in range(gx - 1):
        send_back(t).start()
    recv_g[me_x] = send_g[...]

    for t in range(1, ns):
        s = lax.rem(me_s + t, ns)
        rcopy(tbuf.at[s], tbuf.at[s], sts.at[t], str_.at[s], {"scene": s}).wait_recv()
    ib = c // ns
    wide_l, wide_r = iota((128, ib * c), 1), iota((128, ib * c), 0)
    first = (wide_l >> bits) + me_s * ib
    picks = [
        one_hot(wide_r == (wide_l & (c - 1))),
        one_hot(wide_r == (wide_l & (c - 1)) + c),
        one_hot(wide_r == first + 2 * c),
        one_hot(wide_r == first + 3 * c),
    ]
    g_re = g_im = 0.0
    for s in range(ns):
        o_re, o_im, h_re, h_im = [dot_split(tbuf[s], pick) for pick in picks]
        g_re = g_re + o_re * h_re + o_im * h_im
        g_im = g_im + o_im * h_re - o_re * h_im
    gs_out[0] = g_re[: 9 * MZ]
    gs_out[1] = g_im[: 9 * MZ]

    for g in (14, 15):
        put_local(g).wait()
    for t in range(gx - 1):
        s = peer_x(t)
        rcopy(send_g, recv_g.at[s], sgs.at[t], sgr.at[s], {"gx": s}).wait_recv()

    rows_g = recv_g[...].reshape(kx, cells)

    @pl.loop(0, 4)
    def _(i):
        rows = pl.ds(pl.multiple_of(i * 128, 128), 128)
        b_out[rows, :] = (dot(txh[rows, :], rows_g) + dot(txl[rows, :], rows_g)).astype(BF16)

    for t in range(gx - 1):
        send_planes(t).wait_send()
        send_block(t).wait_send()
        send_back(t).wait_send()
    for t in range(gy - 1):
        send_modes(t).wait_send()
        for copy in send_mode_grads(t):
            copy.wait_send()
    for t in range(1, ns):
        send_table(t).wait_send()


def final_kernel(b_ref, loc_ref, zt_ref, out_ref, zb_ref):
    block = pl.program_id(0)

    @pl.when(block == 0)
    def _():
        zb_ref[...] = jnp.zeros_like(zb_ref)
        for i in range(8):
            for p in range(2):
                zb_ref[i, p * 128 + i * 16 : p * 128 + i * 16 + 16, :] = zt_ref[p]

    half = lax.rem(block, 2) * 4
    lhs = jnp.concatenate([b_ref[0:256, :], b_ref[256:512, :]], axis=1)
    for i in range(4):
        spectral = dot(lhs, zb_ref[half + i])
        out_ref[i] = (spectral + loc_ref[i].astype(F32)).astype(BF16)


def body(field_in, grad_pre, spec_weight, point_weight):
    gx, gy, ns = lax.axis_size("gx"), lax.axis_size("gy"), lax.axis_size("scene")
    c = field_in.shape[1]
    cells = 16 * c
    cc = c * c
    kx = 96 * gx
    norm = float(256 * gx * gy * NZ) ** -0.5
    consts = tables(gx, gy)
    names = ["texp", "m0", "ph", "ty", "phy", "tx", "phx", "rep", "rs", "mk1", "mk2"]
    values = [jnp.asarray(consts[n]) for n in names]
    w = jnp.transpose(spec_weight.reshape(9 * MZ, 2, cc), (1, 0, 2))
    w = jnp.pad(w, ((0, 0), (0, ROWS - 9 * MZ), (0, 0)))
    inputs = [
        field_in.reshape(c, 256, NZ), grad_pre.reshape(c, 256, NZ), w, point_weight, *values
    ]
    vmem = pltpu.VMEM
    dma = pltpu.SemaphoreType.DMA
    nb = 9 * gx
    scratch = [vmem(v.shape, v.dtype) for v in inputs] + [
        vmem((8, 224, NZ), BF16),
        vmem((gx - 1, 2, 112, NZ), BF16), vmem((gx, 2, 112, NZ), BF16),
        vmem((gy, nb, NZ), F32), vmem((gy, nb, NZ), F32),
        vmem((gy - 1, 2 * nb, 128), BF16), vmem((gy, 2 * nb, 128), BF16), vmem((2 * nb, 128), F32),
        vmem((gx, 24, 128), F32), vmem((gx, 24, 128), F32), vmem((ns, ROWS, 128), F32),
        vmem((16, cells), BF16), vmem((gy, 16, cells), BF16), vmem((8, 128), F32), vmem((8 * gy, 128), F32),
        vmem((96, cells), BF16), vmem((gx, 96, cells), BF16),
        vmem((96, 18 * gy), BF16), vmem((96, 18 * gy), BF16), vmem((512, kx), BF16), vmem((512, kx), BF16),
        vmem((cells, cells), BF16), vmem((2, c, 16, NZ), BF16),
        vmem((2, 128 * gx, 128), BF16), vmem((2, 128, cc), BF16), vmem((2, cc, 128), BF16),
        vmem((2, 128, cells), BF16),
        dma((gx,)), dma((gx,)), dma((13,)), dma((2,)),
        *[dma((n,)) for n in (gx, gx, gy, gy, gx, gx, gy, gy, gy, gy, gx, gx, ns, ns)],
    ]
    any_spec = pl.BlockSpec(memory_space=pl.ANY)
    vmem_spec = pl.BlockSpec(memory_space=pltpu.VMEM)
    b, loc, gs = pl.pallas_call(
        functools.partial(comm_kernel, gx, gy, ns, norm),
        out_shape=(
            jax.ShapeDtypeStruct((512, cells), BF16),
            jax.ShapeDtypeStruct((c, 256, NZ), BF16),
            jax.ShapeDtypeStruct((2, 9 * MZ, cc // ns), F32),
        ),
        in_specs=[any_spec] * len(inputs),
        out_specs=(vmem_spec, any_spec, vmem_spec),
        scratch_shapes=scratch,
        compiler_params=pltpu.CompilerParams(
            collective_id=0, has_side_effects=True, vmem_limit_bytes=56 * 1024 * 1024
        ),
        name="spectral_exchange",
    )(*inputs)
    grad = pl.pallas_call(
        final_kernel,
        grid=(c // 4,),
        out_shape=jax.ShapeDtypeStruct((c, 256, NZ), BF16),
        in_specs=[
            pl.BlockSpec((512, 128), lambda i: (0, i // 2)),
            pl.BlockSpec((4, 256, NZ), lambda i: (i, 0, 0)),
            pl.BlockSpec((2, 16, NZ), lambda i: (0, 0, 0)),
        ],
        out_specs=pl.BlockSpec((4, 256, NZ), lambda i: (i, 0, 0)),
        scratch_shapes=[vmem((8, 256, NZ), BF16)],
        compiler_params=pltpu.CompilerParams(vmem_limit_bytes=62 * 1024 * 1024),
        name="inverse_z",
    )(b, loc, jnp.asarray(consts["zb"]))
    grad_field = grad.reshape(field_in.shape)
    grad_spec = jnp.transpose(gs, (1, 0, 2)).reshape(3, 3, MZ, 2, cc // ns)
    return grad_field, grad_spec


def solution(mesh):
    return jax.shard_map(
        body,
        mesh=mesh,
        in_specs=(
            P("scene", None, "gx", "gy", None),
            P("scene", None, "gx", "gy", None),
            P("gx", "gy", None, None, None),
            P(),
        ),
        out_specs=(P("scene", None, "gx", "gy", None), P("gx", "gy", None, None, "scene")),
        check_vma=False,
    )
```

```python
import functools

import jax
import jax.numpy as jnp
import numpy as np
from jax import lax
from jax.experimental import pallas as pl
from jax.experimental.pallas import tpu as pltpu
from jax.sharding import PartitionSpec as P

MZ = 13
NZ = 256
MESH = pl.DeviceIdType.MESH
F32 = jnp.float32
BF16 = jnp.bfloat16
NT_DIMS = (((1,), (1,)), ((), ()))
ROWS = 120


def split_np(value):
    hi = value.astype(np.float32).astype(jnp.bfloat16)
    lo = (value - hi.astype(np.float64)).astype(jnp.bfloat16)
    return hi, lo


def signed(j, m):
    return np.where(j < m // 2, j, j - m)


@functools.lru_cache
def tables(gx, gy):
    mx, my, nx, ny = 3 * gx, 3 * gy, 16 * gx, 16 * gy
    norm = float(nx * ny * NZ) ** -0.5
    out = {}
    k = np.arange(14)
    ang = 2 * np.pi * ((k[:, None] * np.arange(NZ)[None]) % NZ) / NZ
    keep = (k < MZ)[:, None]
    zt = np.stack([np.cos(ang) * keep, -np.sin(ang) * keep])
    out["texp"] = np.repeat(zt.reshape(28, NZ), 4, axis=0).astype(np.float32).astype(jnp.bfloat16)
    fx, fy = signed(np.arange(mx), mx), signed(np.arange(my), my)
    m = np.arange(9)
    a, b = m // 3, m % 3
    kx = fx[3 * np.arange(gx)[None, :] + a[:, None]]
    ky = fy[3 * np.arange(gy)[:, None] + b[None, :]]
    kx = np.broadcast_to(kx[None], (gy, 9, gx)).reshape(gy, -1)
    ky = np.broadcast_to(ky[:, :, None], (gy, 9, gx)).reshape(gy, -1)
    xl, yl = np.repeat(np.arange(16), 16), np.tile(np.arange(16), 16)
    ang = 2 * np.pi * (kx[..., None] * xl / nx + ky[..., None] * yl / ny)
    out["m0"] = np.concatenate(split_np(np.concatenate([np.cos(ang), np.sin(ang)], axis=1)), axis=2)
    ph = np.zeros((gy, 9 * gx, 128), np.float32)
    theta = 2 * np.pi * ((kx[..., None] * np.arange(gx)) % gx) / gx
    phi = 2 * np.pi * ((ky[..., None] * np.arange(gy)) % gy) / gy
    ph[..., 0:gx] = np.cos(theta)
    ph[..., 8 : 8 + gx] = np.sin(theta)
    ph[..., 16 : 16 + gy] = np.cos(phi)
    ph[..., 24 : 24 + gy] = np.sin(phi)
    out["ph"] = ph
    delta = np.array([[0, np.pi / 2], [-np.pi / 2, 0]])
    col_src = np.concatenate([np.repeat(np.arange(gy), 16), np.tile(np.arange(gy), 2)])
    col_p = np.concatenate([np.tile(np.repeat([0, 1], 8), gy), np.repeat([0, 1], gy)])
    col_m = np.concatenate([np.tile(np.arange(8), 2 * gy), np.full(2 * gy, 8)])
    row_p, row_a, row_y = np.repeat([0, 1], 48), np.tile(np.repeat([0, 1, 2], 16), 2), np.tile(np.arange(16), 6)
    col_ky = fy[3 * col_src + col_m % 3]
    ang = 2 * np.pi * col_ky[None] * row_y[:, None] / ny + delta[row_p[:, None], col_p[None]]
    match = row_a[:, None] == (col_m // 3)[None]
    out["ty"] = np.stack([np.cos(ang) * match, np.sin(ang) * match]).astype(np.float32)
    phi = 2 * np.pi * ((np.arange(gy)[:, None] * col_ky[None]) % gy) / gy
    out["phy"] = np.stack([np.cos(phi), np.sin(phi)]).astype(np.float32)
    col = np.arange(96 * gx)
    col_kx = fx[3 * (col // 96) + col // 16 % 3]
    col_p = col // 48 % 2
    row_p, row_x = np.repeat([0, 1], 16), np.tile(np.arange(16), 2)
    ang = 2 * np.pi * col_kx[None] * row_x[:, None] / nx + delta[row_p[:, None], col_p[None]]
    out["tx"] = np.stack([np.cos(ang), np.sin(ang)]).astype(np.float32)
    psi = 2 * np.pi * ((np.arange(gx)[:, None] * col_kx[None]) % gx) / gx
    out["phx"] = np.stack([np.cos(psi), np.sin(psi)]).astype(np.float32)
    rep = np.zeros((2, ROWS, 24))
    rs = np.zeros((2, 32, ROWS))
    mk1 = np.zeros((ROWS, 128))
    mk2 = np.zeros((ROWS, 128))
    for row in range(9 * MZ):
        mode, kz = divmod(row, MZ)
        mk1[row] = (np.arange(128) % 56 // 4 == kz) & (np.arange(128) < 112)
        mk2[row] = np.arange(128) % 16 == kz
        for p in range(2):
            rep[p, row, p * 9 + mode] = 1
            rs[p, p * 8 + mode if mode < 8 else 16 + p, row] = 1
    out["rep"], out["rs"] = rep.astype(jnp.bfloat16), rs.astype(jnp.bfloat16)
    out["mk1"], out["mk2"] = mk1.astype(np.float32), mk2.astype(np.float32)
    k = np.arange(16)
    ang = 2 * np.pi * ((k[:, None] * np.arange(NZ)[None]) % NZ) / NZ
    keep = (k < MZ)[:, None] * norm
    zt = np.stack([np.cos(ang) * keep, -np.sin(ang) * keep])
    out["zb"] = zt.astype(np.float32).astype(jnp.bfloat16)
    return out


def split(value):
    hi = value.astype(BF16)
    return hi, (value - hi.astype(F32)).astype(BF16)


def dot(a, b):
    return jnp.dot(a, b, preferred_element_type=F32)


def dot_split(value, table):
    hi, lo = split(value)
    return dot(hi, table) + dot(lo, table)


def one_hot(cond, value=1.0):
    return jnp.where(cond, value, 0.0).astype(BF16)


def iota(shape, dim):
    return lax.broadcasted_iota(jnp.int32, shape, dim)


def far_offsets(n):
    half = n // 2
    order = []
    for t in range(n - 1):
        order.append(half + t // 2 if t % 2 == 0 else half - (t + 1) // 2)
    return order


def comm_kernel(
    gx, gy, ns, norm,
    xf_hbm, xp_hbm, w_hbm, pw_hbm, texp_hbm, m0_hbm, ph_hbm, ty_hbm, phy_hbm, tx_hbm, phx_hbm,
    rep_hbm, rs_hbm, mk1_hbm, mk2_hbm,
    b_out, loc_hbm, gs_out,
    xf, xp, w, pw, texp, m0, ph, ty, phy, tx, phx, rep, rs, mk1, mk2,
    tj, send1, recv1, acc_c, acc_s, send2, recv2, sum2, send3, recv3, tbuf,
    send_a, recv_a, send_b, recv_b, send_g, recv_g, tyh, tyl, txh, txl, kron, stage,
    sel, orep, selo, rc, w_rows,
    load_f, load_p, load_c, loc_sem,
    s1s, s1r, s2s, s2r, s3s, s3r, sas, sar, sbs, sbr, sgs, sgr, sts, str_,
):
    c = 4 * gx
    cc = c * c
    me_x, me_y, me_s = lax.axis_index("gx"), lax.axis_index("gy"), lax.axis_index("scene")

    half, at_x = me_x // 4, lax.rem(me_x, 4)

    def pick(t, values):
        if isinstance(t, int):
            return values[t]
        result = values[-1]
        for i in range(len(values) - 2, -1, -1):
            result = jnp.where(t == i, values[i], result)
        return result

    def peer_x(t):
        if gx == 8:
            e = pick(t, [2, 0, 1, 3, 2, 1, 3, 0])
            f = pick(t, [1, 1, 1, 1, 0, 0, 0, 0])
            return lax.rem(half + f, 2) * 4 + lax.rem(at_x + e, 4)
        return lax.rem(me_x + 1 + t, gx)

    def peer_y(t):
        return lax.rem(me_y + far_offsets(gy)[t], gy)

    def rcopy(src, dst, ssem, rsem, device):
        return pltpu.make_async_remote_copy(
            src_ref=src, dst_ref=dst, send_sem=ssem, recv_sem=rsem, device_id=device, device_id_type=MESH
        )

    barrier = pltpu.get_barrier_semaphore()
    for t in range(gx - 1):
        pl.semaphore_signal(barrier, inc=1, device_id={"gx": peer_x(t)}, device_id_type=MESH)
    for t in range(gy - 1):
        pl.semaphore_signal(barrier, inc=1, device_id={"gy": peer_y(t)}, device_id_type=MESH)
    for t in range(1, ns):
        pl.semaphore_signal(
            barrier, inc=1, device_id={"scene": lax.rem(me_s + t, ns)}, device_id_type=MESH
        )

    loads = [
        pltpu.make_async_copy(s, d, load_c.at[i])
        for i, (s, d) in enumerate(
            [
                (texp_hbm, texp), (m0_hbm, m0), (ph_hbm, ph), (pw_hbm, pw), (tx_hbm, tx), (phx_hbm, phx),
                (ty_hbm, ty), (phy_hbm, phy), (rep_hbm, rep), (rs_hbm, rs), (mk1_hbm, mk1), (mk2_hbm, mk2),
                (w_hbm, w),
            ]
        )
    ]

    def chunk(hbm, vmem, sems, t):
        rows = pl.ds(peer_x(t) * 4, 4)
        return pltpu.make_async_copy(hbm.at[rows], vmem.at[rows], sems.at[t])

    loads[0].start()
    for t in range(gx):
        chunk(xf_hbm, xf, load_f, t).start()
        chunk(xp_hbm, xp, load_p, t).start()
    for copy in loads[1:]:
        copy.start()

    greeted = gx + gy + ns - 3

    loads[0].wait()
    row_j = iota((112, NZ), 0) & 3
    for j in range(4):
        tj[:, j * NZ : j * NZ + NZ] = jnp.where(row_j == j, texp[...].astype(F32), 0.0).astype(BF16)

    def z_modes(t):
        d = peer_x(t)
        chunk(xf_hbm, xf, load_f, t).wait()
        chunk(xp_hbm, xp, load_p, t).wait()
        parts = []
        for ref in (xf, xp):
            planes = jnp.concatenate([ref[d * 4 + j] for j in range(4)], axis=1)
            parts.append(lax.dot_general(tj[...], planes, NT_DIMS, preferred_element_type=F32))
        rows = [parts[g][p * 56 : p * 56 + 56] for p in range(2) for g in range(2)]
        return jnp.concatenate(rows, axis=0).astype(BF16).reshape(2, 112, NZ)

    def send_planes(t):
        return rcopy(
            send1.at[t], recv1.at[me_x], s1s.at[t], s1r.at[me_x], {"gx": peer_x(t)}
        )

    early = min(4, gx - 1)

    @pl.loop(0, early)
    def _(t):
        send1[t] = z_modes(t)

    pl.semaphore_wait(barrier, greeted)
    for t in range(early):
        send_planes(t).start()

    @pl.loop(early, gx - 1)
    def _(t):
        send1[t] = z_modes(t)
        send_planes(t).start()

    recv1[me_x] = z_modes(gx - 1)

    for copy in loads[1:]:
        copy.wait()
    acc_c[...] = jnp.zeros_like(acc_c)
    acc_s[...] = jnp.zeros_like(acc_s)
    send3[...] = jnp.zeros_like(send3)
    cells = 16 * c
    kx = 96 * gx

    nb = 9 * gx
    lane = iota((nb, 128), 1)

    def column(table, index):
        return jnp.sum(jnp.where(lane == index, table, 0.0), axis=1, keepdims=True)

    def add_source(s):
        cos_t, sin_t = column(ph[0], s), column(ph[0], 8 + s)
        gap = jnp.zeros((16, NZ), BF16)
        block = jnp.concatenate([recv1[s, 0], gap, recv1[s, 1], gap], axis=0)

        block = jnp.concatenate([block, block], axis=1)
        step = min(gy, 4)

        @pl.loop(0, gy // step)
        def _(i):
            tables = m0[pl.ds(i * step, step)].reshape(step * 2 * nb, 2 * NZ)
            part = lax.dot_general(tables, block, NT_DIMS, preferred_element_type=F32)
            for q in range(step):
                part_c = part[2 * q * nb : (2 * q + 1) * nb]
                part_s = part[(2 * q + 1) * nb : (2 * q + 2) * nb]
                acc_c[i * step + q] += cos_t * part_c - sin_t * part_s
                acc_s[i * step + q] += cos_t * part_s + sin_t * part_c

    add_source(me_x)

    @pl.loop(0, gx - 1)
    def _(t):
        s = peer_x(t)
        rcopy(send1.at[t], recv1.at[s], s1s.at[t], s1r.at[s], {"gx": s}).wait_recv()
        add_source(s)

    def modes_for(g):
        cos_t, sin_t = column(ph[g], 16 + me_y), column(ph[g], 24 + me_y)
        total_c, total_s = acc_c[g], acc_s[g]
        turned_c = cos_t * total_c - sin_t * total_s
        turned_s = cos_t * total_s + sin_t * total_c
        re = turned_c[:, :128] + turned_s[:, 128:]
        im = turned_c[:, 128:] - turned_s[:, :128]
        return jnp.concatenate([re, im], axis=0).astype(BF16)

    def send_modes(t):
        return rcopy(send2.at[t], recv2.at[me_y], s2s.at[t], s2r.at[me_y], {"gy": peer_y(t)})

    for t in range(gy - 1):
        send2[t] = modes_for(peer_y(t))
        send_modes(t).start()
    total = modes_for(me_y).astype(F32)

    spread = one_hot(iota((cells, c), 0) >> 4 == iota((cells, c), 1))
    pw_t = lax.dot_general(spread, pw[...], NT_DIMS, preferred_element_type=F32).astype(BF16)
    wide = lax.dot_general(pw_t, spread, NT_DIMS, preferred_element_type=F32)
    same = (iota((cells, cells), 0) & 15) == (iota((cells, cells), 1) & 15)
    kron[...] = jnp.where(same, wide, 0.0).astype(BF16)

    def put_local(g):
        rows = pl.ds(pl.multiple_of(g * 16, 16), 16)
        return pltpu.make_async_copy(stage.at[lax.rem(g, 2)], loc_hbm.at[:, rows, :], loc_sem.at[lax.rem(g, 2)])

    @pl.loop(0, 16)
    def _(g):
        @pl.when(g >= 2)
        def _():
            put_local(g - 2).wait()

        rows = pl.ds(pl.multiple_of(g * 16, 16), 16)
        tile = xp[:, rows, :].reshape(cells, NZ)
        mixed = dot(kron[...], tile)
        stage[lax.rem(g, 2)] = mixed.astype(BF16).reshape(c, 16, NZ)
        put_local(g).start()

    for t in reversed(range(gy - 1)):
        s = peer_y(t)
        rcopy(send2.at[t], recv2.at[s], s2s.at[t], s2r.at[s], {"gy": s}).wait_recv()
        total = total + recv2[s].astype(F32)
    sum2[...] = total

    for g in range(gx):
        send3[g, 0:18, :] = sum2[pl.ds(g, 18, stride=gx), :]

    def send_block(t):
        d = peer_x(t)
        return rcopy(send3.at[d], recv3.at[me_x], s3s.at[t], s3r.at[me_x], {"gx": d})

    for t in range(gx - 1):
        send_block(t).start()
    recv3[me_x] = send3[me_x]

    pairs = w[...].reshape(18 * MZ, cc)
    for p in range(2):
        w_rows[p] = dot(one_hot(iota((ROWS, 18 * MZ), 1) == 2 * iota((ROWS, 18 * MZ), 0) + p), pairs)

    def sel_table(p):
        r, l = iota((gx * 128, 128), 0), iota((gx * 128, 128), 1)
        q = r & 127
        field = q < 56
        k = jnp.where(field, q, q - 56) >> 2
        lane = jnp.where(field, (2 + p) * c, p * c) + 4 * (r >> 7) + (q & 3)
        value = jnp.where(field | (k == 0), norm, 2.0 * norm)
        return jnp.where((l == lane) & (q < 112), value, 0.0).astype(BF16)

    bits = c.bit_length() - 1
    for p in range(2):
        sel[p] = sel_table(p)
        selo[p] = one_hot((iota((cc, 128), 0) >> bits) + p * c == iota((cc, 128), 1))
        orep[p] = one_hot((iota((128, cc), 1) & (c - 1)) + p * c == iota((128, cc), 0))
        rc[p] = one_hot((iota((128, cells), 1) >> 4) + p * c == iota((128, cells), 0))
    ty_now = ty[0] * phy[0, pl.ds(me_y, 1), :] - ty[1] * phy[1, pl.ds(me_y, 1), :]
    tyh[...], tyl[...] = split(ty_now)

    for t in range(gx - 1):
        s = peer_x(t)
        rcopy(send3.at[s], recv3.at[s], s3s.at[t], s3r.at[s], {"gx": s}).wait_recv()

    spectra = jnp.concatenate([recv3[s] for s in range(gx)], axis=1)
    sp_hi, sp_lo = split(spectra)
    mask = jnp.concatenate([mk1[...]] * gx, axis=1)
    table = None
    for p in range(2):
        rows = (dot(rep[p], sp_hi) + dot(rep[p], sp_lo)) * mask
        part = dot_split(rows, sel[p])
        table = part if table is None else table + part
    tbuf[me_s] = table

    def send_table(t):
        return rcopy(
            tbuf.at[me_s], tbuf.at[me_s], sts.at[t], str_.at[me_s], {"scene": lax.rem(me_s + t, ns)}
        )

    for t in range(1, ns):
        send_table(t).start()

    o_re, o_im = dot_split(table, orep[0]), dot_split(table, orep[1])
    grad = dot_split(w_rows[0] * o_re + w_rows[1] * o_im, selo[0])
    grad = grad + dot_split(w_rows[0] * o_im - w_rows[1] * o_re, selo[1])
    grad = grad.astype(BF16)
    mask = jnp.concatenate([mk2[...]] * (cells // 128), axis=1)
    modes = None
    for p in range(2):
        part = dot(rs[p], (dot(grad, rc[p]) * mask).astype(BF16))
        modes = part if modes is None else modes + part
    tiles = cells // 128
    send_a[...] = modes[0:16].astype(BF16)
    for p in range(2):
        for t in range(tiles):
            send_b[p * tiles + t : p * tiles + t + 1, :] = modes[16 + p : 17 + p, t * 128 : t * 128 + 128]

    def send_mode_grads(t):
        d = {"gy": peer_y(t)}
        rows = pl.ds(pl.multiple_of(me_y * 8, 8), 8)
        return (
            rcopy(send_a, recv_a.at[me_y], sas.at[t], sar.at[me_y], d),
            rcopy(send_b, recv_b.at[rows], sbs.at[t], sbr.at[me_y], d),
        )

    for t in range(gy - 1):
        for copy in send_mode_grads(t):
            copy.start()
    recv_a[me_y] = send_a[...]
    recv_b[pl.ds(pl.multiple_of(me_y * 8, 8), 8), :] = send_b[...]
    y_match = (iota((16, kx), 0)) == (iota((16, kx), 1) & 15)
    tx_now = tx[0] * phx[0, pl.ds(me_x, 1), :] - tx[1] * phx[1, pl.ds(me_x, 1), :]
    for r in range(32):
        row = jnp.where(y_match, jnp.broadcast_to(tx_now[r : r + 1], (16, kx)), 0.0)
        txh[r * 16 : r * 16 + 16], txl[r * 16 : r * 16 + 16] = split(row)

    for t in range(gy - 1):
        s = peer_y(t)
        rcopy(send_a, recv_a.at[s], sas.at[t], sar.at[s], {"gy": s}).wait_recv()
        rows = pl.ds(pl.multiple_of(s * 8, 8), 8)
        rcopy(send_b, recv_b.at[rows], sbs.at[t], sbr.at[s], {"gy": s}).wait_recv()

    main = recv_a[...].reshape(16 * gy, cells)
    last = jnp.concatenate(
        [
            jnp.concatenate([recv_b[pl.ds(p * tiles + t, gy, stride=8), :] for p in range(2)], axis=0)
            for t in range(tiles)
        ],
        axis=1,
    ).astype(BF16)
    ka = 16 * gy
    back = dot(tyh[:, :ka], main) + dot(tyl[:, :ka], main)
    back = back + dot(tyh[:, ka:], last) + dot(tyl[:, ka:], last)
    send_g[...] = back.astype(BF16)

    def send_back(t):
        return rcopy(send_g, recv_g.at[me_x], sgs.at[t], sgr.at[me_x], {"gx": peer_x(t)})

    for t in range(gx - 1):
        send_back(t).start()
    recv_g[me_x] = send_g[...]

    for t in range(1, ns):
        s = lax.rem(me_s + t, ns)
        rcopy(tbuf.at[s], tbuf.at[s], sts.at[t], str_.at[s], {"scene": s}).wait_recv()
    ib = c // ns
    wide_l, wide_r = iota((128, ib * c), 1), iota((128, ib * c), 0)
    first = (wide_l >> bits) + me_s * ib
    picks = [
        one_hot(wide_r == (wide_l & (c - 1))),
        one_hot(wide_r == (wide_l & (c - 1)) + c),
        one_hot(wide_r == first + 2 * c),
        one_hot(wide_r == first + 3 * c),
    ]
    g_re = g_im = 0.0
    for s in range(ns):
        o_re, o_im, h_re, h_im = [dot_split(tbuf[s], chosen) for chosen in picks]
        g_re = g_re + o_re * h_re + o_im * h_im
        g_im = g_im + o_im * h_re - o_re * h_im
    gs_out[0] = g_re[: 9 * MZ]
    gs_out[1] = g_im[: 9 * MZ]

    for g in (14, 15):
        put_local(g).wait()
    for t in range(gx - 1):
        s = peer_x(t)
        rcopy(send_g, recv_g.at[s], sgs.at[t], sgr.at[s], {"gx": s}).wait_recv()

    rows_g = recv_g[...].reshape(kx, cells)

    @pl.loop(0, 4)
    def _(i):
        rows = pl.ds(pl.multiple_of(i * 128, 128), 128)
        b_out[rows, :] = (dot(txh[rows, :], rows_g) + dot(txl[rows, :], rows_g)).astype(BF16)

    for t in range(gx - 1):
        send_planes(t).wait_send()
        send_block(t).wait_send()
        send_back(t).wait_send()
    for t in range(gy - 1):
        send_modes(t).wait_send()
        for copy in send_mode_grads(t):
            copy.wait_send()
    for t in range(1, ns):
        send_table(t).wait_send()


def final_kernel(b_ref, loc_ref, zt_ref, out_ref, zb_ref):
    block = pl.program_id(0)

    @pl.when(block == 0)
    def _():
        zb_ref[...] = jnp.zeros_like(zb_ref)
        for i in range(8):
            for p in range(2):
                zb_ref[i, p * 128 + i * 16 : p * 128 + i * 16 + 16, :] = zt_ref[p]

    half = lax.rem(block, 2) * 4
    lhs = jnp.concatenate([b_ref[0:256, :], b_ref[256:512, :]], axis=1)

    def finish(i, spectral):
        out_ref[i] = (spectral + loc_ref[i].astype(F32)).astype(BF16)

    ahead = dot(lhs, zb_ref[half])
    for i in range(4):
        now = ahead
        if i < 3:
            ahead = dot(lhs, zb_ref[half + i + 1])
        finish(i, now)


def body(field_in, grad_pre, spec_weight, point_weight):
    gx, gy, ns = lax.axis_size("gx"), lax.axis_size("gy"), lax.axis_size("scene")
    c = field_in.shape[1]
    cells = 16 * c
    cc = c * c
    kx = 96 * gx
    norm = float(256 * gx * gy * NZ) ** -0.5
    consts = tables(gx, gy)
    names = ["texp", "m0", "ph", "ty", "phy", "tx", "phx", "rep", "rs", "mk1", "mk2"]
    values = [jnp.asarray(consts[n]) for n in names]
    w = spec_weight.reshape(9 * MZ, 2, cc)
    inputs = [
        field_in.reshape(c, 256, NZ), grad_pre.reshape(c, 256, NZ), w, point_weight, *values
    ]
    vmem = pltpu.VMEM
    dma = pltpu.SemaphoreType.DMA
    nb = 9 * gx
    scratch = [vmem(v.shape, v.dtype) for v in inputs] + [
        vmem((112, 4 * NZ), BF16),
        vmem((gx - 1, 2, 112, NZ), BF16), vmem((gx, 2, 112, NZ), BF16),
        vmem((gy, nb, NZ), F32), vmem((gy, nb, NZ), F32),
        vmem((gy - 1, 2 * nb, 128), BF16), vmem((gy, 2 * nb, 128), BF16), vmem((2 * nb, 128), F32),
        vmem((gx, 24, 128), F32), vmem((gx, 24, 128), F32), vmem((ns, ROWS, 128), F32),
        vmem((16, cells), BF16), vmem((gy, 16, cells), BF16), vmem((8, 128), F32), vmem((8 * gy, 128), F32),
        vmem((96, cells), BF16), vmem((gx, 96, cells), BF16),
        vmem((96, 18 * gy), BF16), vmem((96, 18 * gy), BF16), vmem((512, kx), BF16), vmem((512, kx), BF16),
        vmem((cells, cells), BF16), vmem((2, c, 16, NZ), BF16),
        vmem((2, 128 * gx, 128), BF16), vmem((2, 128, cc), BF16), vmem((2, cc, 128), BF16),
        vmem((2, 128, cells), BF16), vmem((2, ROWS, cc), F32),
        dma((gx,)), dma((gx,)), dma((13,)), dma((2,)),
        *[dma((n,)) for n in (gx, gx, gy, gy, gx, gx, gy, gy, gy, gy, gx, gx, ns, ns)],
    ]
    any_spec = pl.BlockSpec(memory_space=pl.ANY)
    vmem_spec = pl.BlockSpec(memory_space=pltpu.VMEM)
    b, loc, gs = pl.pallas_call(
        functools.partial(comm_kernel, gx, gy, ns, norm),
        out_shape=(
            jax.ShapeDtypeStruct((512, cells), BF16),
            jax.ShapeDtypeStruct((c, 256, NZ), BF16),
            jax.ShapeDtypeStruct((2, 9 * MZ, cc // ns), F32),
        ),
        in_specs=[any_spec] * len(inputs),
        out_specs=(vmem_spec, any_spec, vmem_spec),
        scratch_shapes=scratch,
        compiler_params=pltpu.CompilerParams(
            collective_id=0, has_side_effects=True, vmem_limit_bytes=56 * 1024 * 1024
        ),
        name="spectral_exchange",
    )(*inputs)
    grad = pl.pallas_call(
        final_kernel,
        grid=(c // 4,),
        out_shape=jax.ShapeDtypeStruct((c, 256, NZ), BF16),
        in_specs=[
            pl.BlockSpec((512, 128), lambda i: (0, i // 2)),
            pl.BlockSpec((4, 256, NZ), lambda i: (i, 0, 0)),
            pl.BlockSpec((2, 16, NZ), lambda i: (0, 0, 0)),
        ],
        out_specs=pl.BlockSpec((4, 256, NZ), lambda i: (i, 0, 0)),
        scratch_shapes=[vmem((8, 256, NZ), BF16)],
        compiler_params=pltpu.CompilerParams(vmem_limit_bytes=62 * 1024 * 1024),
        name="inverse_z",
    )(b, loc, jnp.asarray(consts["zb"]))
    grad_field = grad.reshape(field_in.shape)
    grad_spec = jnp.transpose(gs, (1, 0, 2)).reshape(3, 3, MZ, 2, cc // ns)
    return grad_field, grad_spec


def solution(mesh):
    return jax.shard_map(
        body,
        mesh=mesh,
        in_specs=(
            P("scene", None, "gx", "gy", None),
            P("scene", None, "gx", "gy", None),
            P("gx", "gy", None, None, None),
            P(),
        ),
        out_specs=(P("scene", None, "gx", "gy", None), P("gx", "gy", None, None, "scene")),
        check_vma=False,
    )
```

```python
import functools

import jax
import jax.numpy as jnp
import numpy as np
from jax import lax
from jax.experimental import pallas as pl
from jax.experimental.pallas import tpu as pltpu
from jax.sharding import PartitionSpec as P

MZ = 13
NZ = 256
MESH = pl.DeviceIdType.MESH
F32 = jnp.float32
BF16 = jnp.bfloat16
NT_DIMS = (((1,), (1,)), ((), ()))
ROWS = 120


def split_np(value):
    hi = value.astype(np.float32).astype(jnp.bfloat16)
    lo = (value - hi.astype(np.float64)).astype(jnp.bfloat16)
    return hi, lo


def signed(j, m):
    return np.where(j < m // 2, j, j - m)


@functools.lru_cache
def tables(gx, gy):
    mx, my, nx, ny = 3 * gx, 3 * gy, 16 * gx, 16 * gy
    norm = float(nx * ny * NZ) ** -0.5
    out = {}
    k = np.arange(14)
    ang = 2 * np.pi * ((k[:, None] * np.arange(NZ)[None]) % NZ) / NZ
    keep = (k < MZ)[:, None]
    zt = np.stack([np.cos(ang) * keep, -np.sin(ang) * keep])
    out["texp"] = np.repeat(zt.reshape(28, NZ), 4, axis=0).astype(np.float32).astype(jnp.bfloat16)
    fx, fy = signed(np.arange(mx), mx), signed(np.arange(my), my)
    m = np.arange(9)
    a, b = m // 3, m % 3
    kx = fx[3 * np.arange(gx)[None, :] + a[:, None]]
    ky = fy[3 * np.arange(gy)[:, None] + b[None, :]]
    kx = np.broadcast_to(kx[None], (gy, 9, gx)).reshape(gy, -1)
    ky = np.broadcast_to(ky[:, :, None], (gy, 9, gx)).reshape(gy, -1)
    xl, yl = np.repeat(np.arange(16), 16), np.tile(np.arange(16), 16)
    ang = 2 * np.pi * (kx[..., None] * xl / nx + ky[..., None] * yl / ny)
    out["m0"] = np.concatenate(split_np(np.concatenate([np.cos(ang), np.sin(ang)], axis=1)), axis=2)
    ph = np.zeros((gy, 9 * gx, 128), np.float32)
    theta = 2 * np.pi * ((kx[..., None] * np.arange(gx)) % gx) / gx
    phi = 2 * np.pi * ((ky[..., None] * np.arange(gy)) % gy) / gy
    ph[..., 0:gx] = np.cos(theta)
    ph[..., 8 : 8 + gx] = np.sin(theta)
    ph[..., 16 : 16 + gy] = np.cos(phi)
    ph[..., 24 : 24 + gy] = np.sin(phi)
    out["ph"] = ph
    delta = np.array([[0, np.pi / 2], [-np.pi / 2, 0]])
    col_src = np.concatenate([np.repeat(np.arange(gy), 16), np.tile(np.arange(gy), 2)])
    col_p = np.concatenate([np.tile(np.repeat([0, 1], 8), gy), np.repeat([0, 1], gy)])
    col_m = np.concatenate([np.tile(np.arange(8), 2 * gy), np.full(2 * gy, 8)])
    row_p, row_a, row_y = np.repeat([0, 1], 48), np.tile(np.repeat([0, 1, 2], 16), 2), np.tile(np.arange(16), 6)
    col_ky = fy[3 * col_src + col_m % 3]
    ang = 2 * np.pi * col_ky[None] * row_y[:, None] / ny + delta[row_p[:, None], col_p[None]]
    match = row_a[:, None] == (col_m // 3)[None]
    out["ty"] = np.stack([np.cos(ang) * match, np.sin(ang) * match]).astype(np.float32)
    phi = 2 * np.pi * ((np.arange(gy)[:, None] * col_ky[None]) % gy) / gy
    out["phy"] = np.stack([np.cos(phi), np.sin(phi)]).astype(np.float32)
    col = np.arange(96 * gx)
    col_kx = fx[3 * (col // 96) + col // 16 % 3]
    col_p = col // 48 % 2
    row_p, row_x = np.repeat([0, 1], 16), np.tile(np.arange(16), 2)
    ang = 2 * np.pi * col_kx[None] * row_x[:, None] / nx + delta[row_p[:, None], col_p[None]]
    out["tx"] = np.stack([np.cos(ang), np.sin(ang)]).astype(np.float32)
    psi = 2 * np.pi * ((np.arange(gx)[:, None] * col_kx[None]) % gx) / gx
    out["phx"] = np.stack([np.cos(psi), np.sin(psi)]).astype(np.float32)
    rep = np.zeros((2, ROWS, 24))
    rs = np.zeros((2, 32, ROWS))
    mk1 = np.zeros((ROWS, 128))
    mk2 = np.zeros((ROWS, 128))
    for row in range(9 * MZ):
        mode, kz = divmod(row, MZ)
        mk1[row] = (np.arange(128) % 56 // 4 == kz) & (np.arange(128) < 112)
        mk2[row] = np.arange(128) % 16 == kz
        for p in range(2):
            rep[p, row, p * 9 + mode] = 1
            rs[p, p * 8 + mode if mode < 8 else 16 + p, row] = 1
    out["rep"], out["rs"] = rep.astype(jnp.bfloat16), rs.astype(jnp.bfloat16)
    out["mk1"], out["mk2"] = mk1.astype(np.float32), mk2.astype(np.float32)
    k = np.arange(16)
    ang = 2 * np.pi * ((k[:, None] * np.arange(NZ)[None]) % NZ) / NZ
    keep = (k < MZ)[:, None] * norm
    zt = np.stack([np.cos(ang) * keep, -np.sin(ang) * keep])
    out["zb"] = zt.astype(np.float32).astype(jnp.bfloat16)
    return out


def split(value):
    hi = value.astype(BF16)
    return hi, (value - hi.astype(F32)).astype(BF16)


def dot(a, b):
    return jnp.dot(a, b, preferred_element_type=F32)


def dot_split(value, table):
    hi, lo = split(value)
    return dot(hi, table) + dot(lo, table)


def one_hot(cond, value=1.0):
    return jnp.where(cond, value, 0.0).astype(BF16)


def iota(shape, dim):
    return lax.broadcasted_iota(jnp.int32, shape, dim)


def far_offsets(n):
    half = n // 2
    order = []
    for t in range(n - 1):
        order.append(half + t // 2 if t % 2 == 0 else half - (t + 1) // 2)
    return order


def comm_kernel(
    gx, gy, ns, norm,
    xf_hbm, xp_hbm, w_hbm, pw_hbm, texp_hbm, m0_hbm, ph_hbm, ty_hbm, phy_hbm, tx_hbm, phx_hbm,
    rep_hbm, rs_hbm, mk1_hbm, mk2_hbm,
    b_out, loc, gs_out,
    xf, xp, w, pw, texp, m0, ph, ty, phy, tx, phx, rep, rs, mk1, mk2,
    tj, send1, recv1, acc_c, acc_s, send2, recv2, sum2, send3, recv3, tbuf,
    send_a, recv_a, send_b, recv_b, send_g, recv_g, tyh, tyl, txh, txl, kron,
    sel, orep, selo, rc, w_rows,
    load_f, load_p, load_c,
    s1s, s1r, s2s, s2r, s3s, s3r, sas, sar, sbs, sbr, sgs, sgr, sts, str_,
):
    c = 4 * gx
    cc = c * c
    me_x, me_y, me_s = lax.axis_index("gx"), lax.axis_index("gy"), lax.axis_index("scene")

    half, at_x = me_x // 4, lax.rem(me_x, 4)

    def pick(t, values):
        if isinstance(t, int):
            return values[t]
        result = values[-1]
        for i in range(len(values) - 2, -1, -1):
            result = jnp.where(t == i, values[i], result)
        return result

    def peer_x(t):
        if gx == 8:
            e = pick(t, [2, 3, 1, 0, 2, 3, 1, 0])
            f = pick(t, [1, 1, 1, 1, 0, 0, 0, 0])
            return lax.rem(half + f, 2) * 4 + lax.rem(at_x + e, 4)
        return lax.rem(me_x + 1 + t, gx)

    def peer_y(t):
        return lax.rem(me_y + far_offsets(gy)[t], gy)

    def rcopy(src, dst, ssem, rsem, device):
        return pltpu.make_async_remote_copy(
            src_ref=src, dst_ref=dst, send_sem=ssem, recv_sem=rsem, device_id=device, device_id_type=MESH
        )

    barrier = pltpu.get_barrier_semaphore()
    for t in range(gx - 1):
        pl.semaphore_signal(barrier, inc=1, device_id={"gx": peer_x(t)}, device_id_type=MESH)
    for t in range(gy - 1):
        pl.semaphore_signal(barrier, inc=1, device_id={"gy": peer_y(t)}, device_id_type=MESH)
    for t in range(1, ns):
        pl.semaphore_signal(
            barrier, inc=1, device_id={"scene": lax.rem(me_s + t, ns)}, device_id_type=MESH
        )

    loads = [
        pltpu.make_async_copy(s, d, load_c.at[i])
        for i, (s, d) in enumerate(
            [
                (texp_hbm, texp), (m0_hbm, m0), (ph_hbm, ph), (pw_hbm, pw), (tx_hbm, tx), (phx_hbm, phx),
                (ty_hbm, ty), (phy_hbm, phy), (rep_hbm, rep), (rs_hbm, rs), (mk1_hbm, mk1), (mk2_hbm, mk2),
                (w_hbm, w),
            ]
        )
    ]

    def chunk(hbm, vmem, sems, t):
        rows = pl.ds(peer_x(t) * 4, 4)
        return pltpu.make_async_copy(hbm.at[rows], vmem.at[rows], sems.at[t])

    loads[0].start()
    for t in range(gx):
        chunk(xf_hbm, xf, load_f, t).start()
        chunk(xp_hbm, xp, load_p, t).start()
    for copy in loads[1:]:
        copy.start()

    greeted = gx + gy + ns - 3

    loads[0].wait()
    row_j = iota((112, NZ), 0) & 3
    for j in range(4):
        tj[:, j * NZ : j * NZ + NZ] = jnp.where(row_j == j, texp[...].astype(F32), 0.0).astype(BF16)

    def z_modes(t):
        d = peer_x(t)
        chunk(xf_hbm, xf, load_f, t).wait()
        chunk(xp_hbm, xp, load_p, t).wait()
        parts = []
        for ref in (xf, xp):
            planes = jnp.concatenate([ref[d * 4 + j] for j in range(4)], axis=1)
            parts.append(lax.dot_general(tj[...], planes, NT_DIMS, preferred_element_type=F32))
        rows = [parts[g][p * 56 : p * 56 + 56] for p in range(2) for g in range(2)]
        return jnp.concatenate(rows, axis=0).astype(BF16).reshape(2, 112, NZ)

    def send_planes(t):
        return rcopy(
            send1.at[t], recv1.at[me_x], s1s.at[t], s1r.at[me_x], {"gx": peer_x(t)}
        )

    early = min(4, gx - 1)

    @pl.loop(0, early)
    def _(t):
        send1[t] = z_modes(t)

    pl.semaphore_wait(barrier, greeted)
    for t in range(early):
        send_planes(t).start()

    @pl.loop(early, gx - 1)
    def _(t):
        send1[t] = z_modes(t)
        send_planes(t).start()

    recv1[me_x] = z_modes(gx - 1)

    for copy in loads[1:]:
        copy.wait()
    acc_c[...] = jnp.zeros_like(acc_c)
    acc_s[...] = jnp.zeros_like(acc_s)
    send3[...] = jnp.zeros_like(send3)
    cells = 16 * c
    kx = 96 * gx

    pairs = w[...].reshape(18 * MZ, cc)
    for p in range(2):
        w_rows[p] = dot(one_hot(iota((ROWS, 18 * MZ), 1) == 2 * iota((ROWS, 18 * MZ), 0) + p), pairs)

    def sel_table(p):
        r, l = iota((gx * 128, 128), 0), iota((gx * 128, 128), 1)
        q = r & 127
        field = q < 56
        k = jnp.where(field, q, q - 56) >> 2
        lane = jnp.where(field, (2 + p) * c, p * c) + 4 * (r >> 7) + (q & 3)
        value = jnp.where(field | (k == 0), norm, 2.0 * norm)
        return jnp.where((l == lane) & (q < 112), value, 0.0).astype(BF16)

    bits = c.bit_length() - 1
    for p in range(2):
        sel[p] = sel_table(p)
        selo[p] = one_hot((iota((cc, 128), 0) >> bits) + p * c == iota((cc, 128), 1))
        orep[p] = one_hot((iota((128, cc), 1) & (c - 1)) + p * c == iota((128, cc), 0))
        rc[p] = one_hot((iota((128, cells), 1) >> 4) + p * c == iota((128, cells), 0))
    ty_now = ty[0] * phy[0, pl.ds(me_y, 1), :] - ty[1] * phy[1, pl.ds(me_y, 1), :]
    tyh[...], tyl[...] = split(ty_now)

    nb = 9 * gx
    lane = iota((nb, 128), 1)

    def column(table, index):
        return jnp.sum(jnp.where(lane == index, table, 0.0), axis=1, keepdims=True)

    def add_source(s):
        cos_t, sin_t = column(ph[0], s), column(ph[0], 8 + s)
        gap = jnp.zeros((16, NZ), BF16)
        block = jnp.concatenate([recv1[s, 0], gap, recv1[s, 1], gap], axis=0)

        block = jnp.concatenate([block, block], axis=1)
        step = min(gy, 4)

        @pl.loop(0, gy // step)
        def _(i):
            tables = m0[pl.ds(i * step, step)].reshape(step * 2 * nb, 2 * NZ)
            part = lax.dot_general(tables, block, NT_DIMS, preferred_element_type=F32)
            for q in range(step):
                part_c = part[2 * q * nb : (2 * q + 1) * nb]
                part_s = part[(2 * q + 1) * nb : (2 * q + 2) * nb]
                acc_c[i * step + q] += cos_t * part_c - sin_t * part_s
                acc_s[i * step + q] += cos_t * part_s + sin_t * part_c

    add_source(me_x)

    @pl.loop(0, gx - 1)
    def _(t):
        s = peer_x(t)
        rcopy(send1.at[t], recv1.at[s], s1s.at[t], s1r.at[s], {"gx": s}).wait_recv()
        add_source(s)

    def modes_for(g):
        cos_t, sin_t = column(ph[g], 16 + me_y), column(ph[g], 24 + me_y)
        total_c, total_s = acc_c[g], acc_s[g]
        turned_c = cos_t * total_c - sin_t * total_s
        turned_s = cos_t * total_s + sin_t * total_c
        re = turned_c[:, :128] + turned_s[:, 128:]
        im = turned_c[:, 128:] - turned_s[:, :128]
        return jnp.concatenate([re, im], axis=0).astype(BF16)

    def send_modes(t):
        return rcopy(send2.at[t], recv2.at[me_y], s2s.at[t], s2r.at[me_y], {"gy": peer_y(t)})

    for t in range(gy - 1):
        send2[t] = modes_for(peer_y(t))
        send_modes(t).start()
    total = modes_for(me_y).astype(F32)

    spread = one_hot(iota((cells, c), 0) >> 4 == iota((cells, c), 1))
    pw_t = lax.dot_general(spread, pw[...], NT_DIMS, preferred_element_type=F32).astype(BF16)
    wide = lax.dot_general(pw_t, spread, NT_DIMS, preferred_element_type=F32)
    same = (iota((cells, cells), 0) & 15) == (iota((cells, cells), 1) & 15)
    kron[...] = jnp.where(same, wide, 0.0).astype(BF16)

    @pl.loop(0, 16)
    def _(g):
        rows = pl.ds(pl.multiple_of(g * 16, 16), 16)
        mixed = dot(kron[...], xp[:, rows, :].reshape(cells, NZ))
        loc[:, rows, :] = mixed.astype(BF16).reshape(c, 16, NZ)

    for t in reversed(range(gy - 1)):
        s = peer_y(t)
        rcopy(send2.at[t], recv2.at[s], s2s.at[t], s2r.at[s], {"gy": s}).wait_recv()
        total = total + recv2[s].astype(F32)
    sum2[...] = total

    for g in range(gx):
        send3[g, 0:18, :] = sum2[pl.ds(g, 18, stride=gx), :]

    def send_block(t):
        d = peer_x(t)
        return rcopy(send3.at[d], recv3.at[me_x], s3s.at[t], s3r.at[me_x], {"gx": d})

    for t in range(gx - 1):
        send_block(t).start()
    recv3[me_x] = send3[me_x]

    for t in range(gx - 1):
        s = peer_x(t)
        rcopy(send3.at[s], recv3.at[s], s3s.at[t], s3r.at[s], {"gx": s}).wait_recv()

    spectra = jnp.concatenate([recv3[s] for s in range(gx)], axis=1)
    sp_hi, sp_lo = split(spectra)
    mask = jnp.concatenate([mk1[...]] * gx, axis=1)
    table = None
    for p in range(2):
        rows = (dot(rep[p], sp_hi) + dot(rep[p], sp_lo)) * mask
        part = dot_split(rows, sel[p])
        table = part if table is None else table + part
    tbuf[me_s] = table

    def send_table(t):
        return rcopy(
            tbuf.at[me_s], tbuf.at[me_s], sts.at[t], str_.at[me_s], {"scene": lax.rem(me_s + t, ns)}
        )

    for t in range(1, ns):
        send_table(t).start()

    o_re, o_im = dot_split(table, orep[0]), dot_split(table, orep[1])
    grad = dot_split(w_rows[0] * o_re + w_rows[1] * o_im, selo[0])
    grad = grad + dot_split(w_rows[0] * o_im - w_rows[1] * o_re, selo[1])
    grad = grad.astype(BF16)
    mask = jnp.concatenate([mk2[...]] * (cells // 128), axis=1)
    modes = None
    for p in range(2):
        part = dot(rs[p], (dot(grad, rc[p]) * mask).astype(BF16))
        modes = part if modes is None else modes + part
    tiles = cells // 128
    send_a[...] = modes[0:16].astype(BF16)
    for p in range(2):
        for t in range(tiles):
            send_b[p * tiles + t : p * tiles + t + 1, :] = modes[16 + p : 17 + p, t * 128 : t * 128 + 128]

    def send_mode_grads(t):
        d = {"gy": peer_y(t)}
        rows = pl.ds(pl.multiple_of(me_y * 8, 8), 8)
        return (
            rcopy(send_a, recv_a.at[me_y], sas.at[t], sar.at[me_y], d),
            rcopy(send_b, recv_b.at[rows], sbs.at[t], sbr.at[me_y], d),
        )

    for t in range(gy - 1):
        for copy in send_mode_grads(t):
            copy.start()
    recv_a[me_y] = send_a[...]
    recv_b[pl.ds(pl.multiple_of(me_y * 8, 8), 8), :] = send_b[...]
    y_match = (iota((16, kx), 0)) == (iota((16, kx), 1) & 15)
    tx_now = tx[0] * phx[0, pl.ds(me_x, 1), :] - tx[1] * phx[1, pl.ds(me_x, 1), :]
    for r in range(32):
        row = jnp.where(y_match, jnp.broadcast_to(tx_now[r : r + 1], (16, kx)), 0.0)
        txh[r * 16 : r * 16 + 16], txl[r * 16 : r * 16 + 16] = split(row)

    for t in range(gy - 1):
        s = peer_y(t)
        rcopy(send_a, recv_a.at[s], sas.at[t], sar.at[s], {"gy": s}).wait_recv()
        rows = pl.ds(pl.multiple_of(s * 8, 8), 8)
        rcopy(send_b, recv_b.at[rows], sbs.at[t], sbr.at[s], {"gy": s}).wait_recv()

    main = recv_a[...].reshape(16 * gy, cells)
    last = jnp.concatenate(
        [
            jnp.concatenate([recv_b[pl.ds(p * tiles + t, gy, stride=8), :] for p in range(2)], axis=0)
            for t in range(tiles)
        ],
        axis=1,
    ).astype(BF16)
    ka = 16 * gy
    back = dot(tyh[:, :ka], main) + dot(tyl[:, :ka], main)
    back = back + dot(tyh[:, ka:], last) + dot(tyl[:, ka:], last)
    send_g[...] = back.astype(BF16)

    def send_back(t):
        return rcopy(send_g, recv_g.at[me_x], sgs.at[t], sgr.at[me_x], {"gx": peer_x(t)})

    for t in range(gx - 1):
        send_back(t).start()
    recv_g[me_x] = send_g[...]

    for t in range(1, ns):
        s = lax.rem(me_s + t, ns)
        rcopy(tbuf.at[s], tbuf.at[s], sts.at[t], str_.at[s], {"scene": s}).wait_recv()
    ib = c // ns
    wide_l, wide_r = iota((128, ib * c), 1), iota((128, ib * c), 0)
    first = (wide_l >> bits) + me_s * ib
    picks = [
        one_hot(wide_r == (wide_l & (c - 1))),
        one_hot(wide_r == (wide_l & (c - 1)) + c),
        one_hot(wide_r == first + 2 * c),
        one_hot(wide_r == first + 3 * c),
    ]
    g_re = g_im = 0.0
    for s in range(ns):
        o_re, o_im, h_re, h_im = [dot_split(tbuf[s], chosen) for chosen in picks]
        g_re = g_re + o_re * h_re + o_im * h_im
        g_im = g_im + o_im * h_re - o_re * h_im
    gs_out[0] = g_re[: 9 * MZ]
    gs_out[1] = g_im[: 9 * MZ]

    for t in range(gx - 1):
        s = peer_x(t)
        rcopy(send_g, recv_g.at[s], sgs.at[t], sgr.at[s], {"gx": s}).wait_recv()

    rows_g = recv_g[...].reshape(kx, cells)

    @pl.loop(0, 4)
    def _(i):
        rows = pl.ds(pl.multiple_of(i * 128, 128), 128)
        b_out[rows, :] = (dot(txh[rows, :], rows_g) + dot(txl[rows, :], rows_g)).astype(BF16)

    for t in range(gx - 1):
        send_planes(t).wait_send()
        send_block(t).wait_send()
        send_back(t).wait_send()
    for t in range(gy - 1):
        send_modes(t).wait_send()
        for copy in send_mode_grads(t):
            copy.wait_send()
    for t in range(1, ns):
        send_table(t).wait_send()


def final_kernel(b_ref, loc_ref, zt_ref, out_ref, zb_ref):
    block = pl.program_id(0)

    @pl.when(block == 0)
    def _():
        zb_ref[...] = jnp.zeros_like(zb_ref)
        for i in range(8):
            for p in range(2):
                zb_ref[i, p * 128 + i * 16 : p * 128 + i * 16 + 16, :] = zt_ref[p]

    half = lax.rem(block, 2) * 4
    lanes = pl.ds(pl.multiple_of(block // 2 * 128, 128), 128)
    lhs = jnp.concatenate([b_ref[0:256, lanes], b_ref[256:512, lanes]], axis=1)

    def finish(i, spectral):
        out_ref[i] = (spectral + loc_ref[block * 4 + i].astype(F32)).astype(BF16)

    ahead = dot(lhs, zb_ref[half])
    for i in range(4):
        now = ahead
        if i < 3:
            ahead = dot(lhs, zb_ref[half + i + 1])
        finish(i, now)


def body(field_in, grad_pre, spec_weight, point_weight):
    gx, gy, ns = lax.axis_size("gx"), lax.axis_size("gy"), lax.axis_size("scene")
    c = field_in.shape[1]
    cells = 16 * c
    cc = c * c
    kx = 96 * gx
    norm = float(256 * gx * gy * NZ) ** -0.5
    consts = tables(gx, gy)
    names = ["texp", "m0", "ph", "ty", "phy", "tx", "phx", "rep", "rs", "mk1", "mk2"]
    values = [jnp.asarray(consts[n]) for n in names]
    w = spec_weight.reshape(9 * MZ, 2, cc)
    inputs = [
        field_in.reshape(c, 256, NZ), grad_pre.reshape(c, 256, NZ), w, point_weight, *values
    ]
    vmem = pltpu.VMEM
    dma = pltpu.SemaphoreType.DMA
    nb = 9 * gx
    scratch = [vmem(v.shape, v.dtype) for v in inputs] + [
        vmem((112, 4 * NZ), BF16),
        vmem((gx - 1, 2, 112, NZ), BF16), vmem((gx, 2, 112, NZ), BF16),
        vmem((gy, nb, NZ), F32), vmem((gy, nb, NZ), F32),
        vmem((gy - 1, 2 * nb, 128), BF16), vmem((gy, 2 * nb, 128), BF16), vmem((2 * nb, 128), F32),
        vmem((gx, 24, 128), F32), vmem((gx, 24, 128), F32), vmem((ns, ROWS, 128), F32),
        vmem((16, cells), BF16), vmem((gy, 16, cells), BF16), vmem((8, 128), F32), vmem((8 * gy, 128), F32),
        vmem((96, cells), BF16), vmem((gx, 96, cells), BF16),
        vmem((96, 18 * gy), BF16), vmem((96, 18 * gy), BF16), vmem((512, kx), BF16), vmem((512, kx), BF16),
        vmem((cells, cells), BF16),
        vmem((2, 128 * gx, 128), BF16), vmem((2, 128, cc), BF16), vmem((2, cc, 128), BF16),
        vmem((2, 128, cells), BF16), vmem((2, ROWS, cc), F32),
        dma((gx,)), dma((gx,)), dma((13,)),
        *[dma((n,)) for n in (gx, gx, gy, gy, gx, gx, gy, gy, gy, gy, gx, gx, ns, ns)],
    ]
    hbm_spec = pl.BlockSpec(memory_space=pl.ANY)
    vmem_spec = pl.BlockSpec(memory_space=pltpu.VMEM)
    b, loc, gs = pl.pallas_call(
        functools.partial(comm_kernel, gx, gy, ns, norm),
        out_shape=(
            jax.ShapeDtypeStruct((512, cells), BF16),
            jax.ShapeDtypeStruct((c, 256, NZ), BF16),
            jax.ShapeDtypeStruct((2, 9 * MZ, cc // ns), F32),
        ),
        in_specs=[hbm_spec] * len(inputs),
        out_specs=(vmem_spec, vmem_spec, vmem_spec),
        scratch_shapes=scratch,
        compiler_params=pltpu.CompilerParams(
            collective_id=0, has_side_effects=True, vmem_limit_bytes=40 * 1024 * 1024
        ),
        name="spectral_exchange",
    )(*[pltpu.with_memory_space_constraint(v, pltpu.HBM) for v in inputs])
    grad = pl.pallas_call(
        final_kernel,
        grid=(c // 4,),
        out_shape=jax.ShapeDtypeStruct((c, 256, NZ), BF16),
        in_specs=[
            vmem_spec,
            vmem_spec,
            vmem_spec,
        ],
        out_specs=pl.BlockSpec((4, 256, NZ), lambda i: (i, 0, 0)),
        scratch_shapes=[vmem((8, 256, NZ), BF16)],
        compiler_params=pltpu.CompilerParams(vmem_limit_bytes=24 * 1024 * 1024),
        name="inverse_z",
    )(b, loc, jnp.asarray(consts["zb"]))
    grad_field = grad.reshape(field_in.shape)
    grad_spec = jnp.transpose(gs, (1, 0, 2)).reshape(3, 3, MZ, 2, cc // ns)
    return grad_field, grad_spec


def solution(mesh):
    return jax.shard_map(
        body,
        mesh=mesh,
        in_specs=(
            P("scene", None, "gx", "gy", None),
            P("scene", None, "gx", "gy", None),
            P("gx", "gy", None, None, None),
            P(),
        ),
        out_specs=(P("scene", None, "gx", "gy", None), P("gx", "gy", None, None, "scene")),
        check_vma=False,
    )
```

```python
import functools

import jax
import jax.numpy as jnp
import numpy as np
from jax import lax
from jax.experimental import pallas as pl
from jax.experimental.pallas import tpu as pltpu
from jax.sharding import PartitionSpec as P

MZ = 13
NZ = 256
MESH = pl.DeviceIdType.MESH
F32 = jnp.float32
BF16 = jnp.bfloat16
NT_DIMS = (((1,), (1,)), ((), ()))
ROWS = 120


def split_np(value):
    hi = value.astype(np.float32).astype(jnp.bfloat16)
    lo = (value - hi.astype(np.float64)).astype(jnp.bfloat16)
    return hi, lo


def signed(j, m):
    return np.where(j < m // 2, j, j - m)


@functools.lru_cache
def tables(gx, gy):
    mx, my, nx, ny = 3 * gx, 3 * gy, 16 * gx, 16 * gy
    norm = float(nx * ny * NZ) ** -0.5
    out = {}
    k = np.arange(14)
    ang = 2 * np.pi * ((k[:, None] * np.arange(NZ)[None]) % NZ) / NZ
    keep = (k < MZ)[:, None]
    zt = np.stack([np.cos(ang) * keep, -np.sin(ang) * keep])
    out["texp"] = np.repeat(zt.reshape(28, NZ), 4, axis=0).astype(np.float32).astype(jnp.bfloat16)
    fx, fy = signed(np.arange(mx), mx), signed(np.arange(my), my)
    m = np.arange(9)
    a, b = m // 3, m % 3
    kx = fx[3 * np.arange(gx)[None, :] + a[:, None]]
    ky = fy[3 * np.arange(gy)[:, None] + b[None, :]]
    kx = np.broadcast_to(kx[None], (gy, 9, gx)).reshape(gy, -1)
    ky = np.broadcast_to(ky[:, :, None], (gy, 9, gx)).reshape(gy, -1)
    xl, yl = np.repeat(np.arange(16), 16), np.tile(np.arange(16), 16)
    ang = 2 * np.pi * (kx[..., None] * xl / nx + ky[..., None] * yl / ny)
    out["m0"] = np.concatenate(split_np(np.concatenate([np.cos(ang), np.sin(ang)], axis=1)), axis=2)
    ph = np.zeros((gy, 9 * gx, 128), np.float32)
    theta = 2 * np.pi * ((kx[..., None] * np.arange(gx)) % gx) / gx
    phi = 2 * np.pi * ((ky[..., None] * np.arange(gy)) % gy) / gy
    ph[..., 0:gx] = np.cos(theta)
    ph[..., 8 : 8 + gx] = np.sin(theta)
    ph[..., 16 : 16 + gy] = np.cos(phi)
    ph[..., 24 : 24 + gy] = np.sin(phi)
    out["ph"] = ph
    delta = np.array([[0, np.pi / 2], [-np.pi / 2, 0]])
    col_src = np.concatenate([np.repeat(np.arange(gy), 16), np.tile(np.arange(gy), 2)])
    col_p = np.concatenate([np.tile(np.repeat([0, 1], 8), gy), np.repeat([0, 1], gy)])
    col_m = np.concatenate([np.tile(np.arange(8), 2 * gy), np.full(2 * gy, 8)])
    row_p, row_a, row_y = np.repeat([0, 1], 48), np.tile(np.repeat([0, 1, 2], 16), 2), np.tile(np.arange(16), 6)
    col_ky = fy[3 * col_src + col_m % 3]
    ang = 2 * np.pi * col_ky[None] * row_y[:, None] / ny + delta[row_p[:, None], col_p[None]]
    match = row_a[:, None] == (col_m // 3)[None]
    out["ty"] = np.stack([np.cos(ang) * match, np.sin(ang) * match]).astype(np.float32)
    phi = 2 * np.pi * ((np.arange(gy)[:, None] * col_ky[None]) % gy) / gy
    out["phy"] = np.stack([np.cos(phi), np.sin(phi)]).astype(np.float32)
    col = np.arange(128 * gx)
    used = col % 128 < 96
    col_kx = fx[3 * (col // 128) + col % 128 // 16 % 3]
    col_p = np.where(used, col % 128 // 48, 0)
    row_p, row_x = np.repeat([0, 1], 16), np.tile(np.arange(16), 2)
    ang = 2 * np.pi * col_kx[None] * row_x[:, None] / nx + delta[row_p[:, None], col_p[None]]
    out["tx"] = np.stack([np.cos(ang) * used, np.sin(ang) * used]).astype(np.float32)
    psi = 2 * np.pi * ((np.arange(gx)[:, None] * col_kx[None]) % gx) / gx
    out["phx"] = np.stack([np.cos(psi), np.sin(psi)]).astype(np.float32)
    rep = np.zeros((2, ROWS, 24))
    rs = np.zeros((2, 32, ROWS))
    mk1 = np.zeros((ROWS, 128))
    mk2 = np.zeros((ROWS, 128))
    for row in range(9 * MZ):
        mode, kz = divmod(row, MZ)
        mk1[row] = (np.arange(128) % 56 // 4 == kz) & (np.arange(128) < 112)
        mk2[row] = np.arange(128) % 16 == kz
        for p in range(2):
            rep[p, row, p * 9 + mode] = 1
            rs[p, p * 8 + mode if mode < 8 else 16 + p, row] = 1
    out["rep"], out["rs"] = rep.astype(jnp.bfloat16), rs.astype(jnp.bfloat16)
    out["mk1"], out["mk2"] = mk1.astype(np.float32), mk2.astype(np.float32)
    k = np.arange(16)
    ang = 2 * np.pi * ((k[:, None] * np.arange(NZ)[None]) % NZ) / NZ
    keep = (k < MZ)[:, None] * norm
    zt = np.stack([np.cos(ang) * keep, -np.sin(ang) * keep])
    out["zb"] = zt.astype(np.float32).astype(jnp.bfloat16)
    return out


def split(value):
    hi = value.astype(BF16)
    return hi, (value - hi.astype(F32)).astype(BF16)


def dot(a, b):
    return jnp.dot(a, b, preferred_element_type=F32)


def dot_split(value, table):
    hi, lo = split(value)
    return dot(hi, table) + dot(lo, table)


def one_hot(cond, value=1.0):
    return jnp.where(cond, value, 0.0).astype(BF16)


def iota(shape, dim):
    return lax.broadcasted_iota(jnp.int32, shape, dim)


def far_offsets(n):
    half = n // 2
    order = []
    for t in range(n - 1):
        order.append(half + t // 2 if t % 2 == 0 else half - (t + 1) // 2)
    return order


def comm_kernel(
    gx, gy, ns, norm,
    xf_hbm, xp_hbm, w_hbm, pw_hbm, texp_hbm, m0_hbm, ph_hbm, ty_hbm, phy_hbm, tx_hbm, phx_hbm,
    rep_hbm, rs_hbm, mk1_hbm, mk2_hbm,
    b_out, loc, gs_out,
    xf, xp, w, pw, texp, m0, ph, ty, phy, tx, phx, rep, rs, mk1, mk2,
    tj, send1, recv1, acc_c, acc_s, send2, recv2, sum2, send3, recv3, tbuf,
    send_a, recv_a, send_b, recv_b, send_g, recv_g, tyh, tyl, txt, b_sum, kron,
    sel, orep, selo, rc, w_rows,
    load_f, load_p, load_c,
    s1s, s1r, s2s, s2r, s3s, s3r, sas, sar, sbs, sbr, sgs, sgr, sts, str_,
):
    c = 4 * gx
    cc = c * c
    me_x, me_y, me_s = lax.axis_index("gx"), lax.axis_index("gy"), lax.axis_index("scene")

    half, at_x = me_x // 4, lax.rem(me_x, 4)

    def pick(t, values):
        if isinstance(t, int):
            return values[t]
        result = values[-1]
        for i in range(len(values) - 2, -1, -1):
            result = jnp.where(t == i, values[i], result)
        return result

    def peer_x(t):
        if gx == 8:
            e = pick(t, [2, 3, 1, 0, 2, 3, 1, 0])
            f = pick(t, [1, 1, 1, 1, 0, 0, 0, 0])
            return lax.rem(half + f, 2) * 4 + lax.rem(at_x + e, 4)
        return lax.rem(me_x + 1 + t, gx)

    def peer_y(t):
        return lax.rem(me_y + far_offsets(gy)[t], gy)

    def rcopy(src, dst, ssem, rsem, device):
        return pltpu.make_async_remote_copy(
            src_ref=src, dst_ref=dst, send_sem=ssem, recv_sem=rsem, device_id=device, device_id_type=MESH
        )

    barrier = pltpu.get_barrier_semaphore()
    for t in range(gx - 1):
        pl.semaphore_signal(barrier, inc=1, device_id={"gx": peer_x(t)}, device_id_type=MESH)
    for t in range(gy - 1):
        pl.semaphore_signal(barrier, inc=1, device_id={"gy": peer_y(t)}, device_id_type=MESH)
    for t in range(1, ns):
        pl.semaphore_signal(
            barrier, inc=1, device_id={"scene": lax.rem(me_s + t, ns)}, device_id_type=MESH
        )

    loads = [
        pltpu.make_async_copy(s, d, load_c.at[i])
        for i, (s, d) in enumerate(
            [
                (texp_hbm, texp), (m0_hbm, m0), (ph_hbm, ph), (pw_hbm, pw), (tx_hbm, tx), (phx_hbm, phx),
                (ty_hbm, ty), (phy_hbm, phy), (rep_hbm, rep), (rs_hbm, rs), (mk1_hbm, mk1), (mk2_hbm, mk2),
                (w_hbm, w),
            ]
        )
    ]

    def chunk(hbm, vmem, sems, t):
        rows = pl.ds(peer_x(t) * 4, 4)
        return pltpu.make_async_copy(hbm.at[rows], vmem.at[rows], sems.at[t])

    loads[0].start()
    for t in range(gx):
        chunk(xf_hbm, xf, load_f, t).start()
        chunk(xp_hbm, xp, load_p, t).start()
    for copy in loads[1:]:
        copy.start()

    greeted = gx + gy + ns - 3

    loads[0].wait()
    row_j = iota((112, NZ), 0) & 3
    for j in range(4):
        tj[:, j * NZ : j * NZ + NZ] = jnp.where(row_j == j, texp[...].astype(F32), 0.0).astype(BF16)

    def z_modes(t):
        d = peer_x(t)
        chunk(xf_hbm, xf, load_f, t).wait()
        chunk(xp_hbm, xp, load_p, t).wait()
        parts = []
        for ref in (xf, xp):
            planes = jnp.concatenate([ref[d * 4 + j] for j in range(4)], axis=1)
            parts.append(lax.dot_general(tj[...], planes, NT_DIMS, preferred_element_type=F32))
        rows = [parts[g][p * 56 : p * 56 + 56] for p in range(2) for g in range(2)]
        return jnp.concatenate(rows, axis=0).astype(BF16).reshape(2, 112, NZ)

    def send_planes(t):
        return rcopy(
            send1.at[t], recv1.at[me_x], s1s.at[t], s1r.at[me_x], {"gx": peer_x(t)}
        )

    early = min(4, gx - 1)

    @pl.loop(0, early)
    def _(t):
        send1[t] = z_modes(t)

    pl.semaphore_wait(barrier, greeted)
    for t in range(early):
        send_planes(t).start()

    @pl.loop(early, gx - 1)
    def _(t):
        send1[t] = z_modes(t)
        send_planes(t).start()

    recv1[me_x] = z_modes(gx - 1)

    for copy in loads[1:]:
        copy.wait()
    acc_c[...] = jnp.zeros_like(acc_c)
    acc_s[...] = jnp.zeros_like(acc_s)
    send3[...] = jnp.zeros_like(send3)
    cells = 16 * c
    kx = 128 * gx

    pairs = w[...].reshape(18 * MZ, cc)
    for p in range(2):
        w_rows[p] = dot(one_hot(iota((ROWS, 18 * MZ), 1) == 2 * iota((ROWS, 18 * MZ), 0) + p), pairs)

    def sel_table(p):
        r, l = iota((gx * 128, 128), 0), iota((gx * 128, 128), 1)
        q = r & 127
        field = q < 56
        k = jnp.where(field, q, q - 56) >> 2
        lane = jnp.where(field, (2 + p) * c, p * c) + 4 * (r >> 7) + (q & 3)
        value = jnp.where(field | (k == 0), norm, 2.0 * norm)
        return jnp.where((l == lane) & (q < 112), value, 0.0).astype(BF16)

    bits = c.bit_length() - 1
    for p in range(2):
        sel[p] = sel_table(p)
        selo[p] = one_hot((iota((cc, 128), 0) >> bits) + p * c == iota((cc, 128), 1))
        orep[p] = one_hot((iota((128, cc), 1) & (c - 1)) + p * c == iota((128, cc), 0))
        rc[p] = one_hot((iota((128, cells), 1) >> 4) + p * c == iota((128, cells), 0))
    ty_now = ty[0] * phy[0, pl.ds(me_y, 1), :] - ty[1] * phy[1, pl.ds(me_y, 1), :]
    tyh[...], tyl[...] = split(ty_now)

    nb = 9 * gx
    lane = iota((nb, 128), 1)

    def column(table, index):
        return jnp.sum(jnp.where(lane == index, table, 0.0), axis=1, keepdims=True)

    def add_source(s):
        cos_t, sin_t = column(ph[0], s), column(ph[0], 8 + s)
        gap = jnp.zeros((16, NZ), BF16)
        block = jnp.concatenate([recv1[s, 0], gap, recv1[s, 1], gap], axis=0)

        block = jnp.concatenate([block, block], axis=1)
        step = min(gy, 4)

        @pl.loop(0, gy // step)
        def _(i):
            tables = m0[pl.ds(i * step, step)].reshape(step * 2 * nb, 2 * NZ)
            part = lax.dot_general(tables, block, NT_DIMS, preferred_element_type=F32)
            for q in range(step):
                part_c = part[2 * q * nb : (2 * q + 1) * nb]
                part_s = part[(2 * q + 1) * nb : (2 * q + 2) * nb]
                acc_c[i * step + q] += cos_t * part_c - sin_t * part_s
                acc_s[i * step + q] += cos_t * part_s + sin_t * part_c

    add_source(me_x)

    @pl.loop(0, gx - 1)
    def _(t):
        s = peer_x(t)
        rcopy(send1.at[t], recv1.at[s], s1s.at[t], s1r.at[s], {"gx": s}).wait_recv()
        add_source(s)

    def modes_for(g):
        cos_t, sin_t = column(ph[g], 16 + me_y), column(ph[g], 24 + me_y)
        total_c, total_s = acc_c[g], acc_s[g]
        turned_c = cos_t * total_c - sin_t * total_s
        turned_s = cos_t * total_s + sin_t * total_c
        re = turned_c[:, :128] + turned_s[:, 128:]
        im = turned_c[:, 128:] - turned_s[:, :128]
        return jnp.concatenate([re, im], axis=0).astype(BF16)

    def send_modes(t):
        return rcopy(send2.at[t], recv2.at[me_y], s2s.at[t], s2r.at[me_y], {"gy": peer_y(t)})

    for t in range(gy - 1):
        send2[t] = modes_for(peer_y(t))
        send_modes(t).start()
    total = modes_for(me_y).astype(F32)

    spread = one_hot(iota((cells, c), 0) >> 4 == iota((cells, c), 1))
    pw_t = lax.dot_general(spread, pw[...], NT_DIMS, preferred_element_type=F32).astype(BF16)
    wide = lax.dot_general(pw_t, spread, NT_DIMS, preferred_element_type=F32)
    same = (iota((cells, cells), 0) & 15) == (iota((cells, cells), 1) & 15)
    kron[...] = jnp.where(same, wide, 0.0).astype(BF16)

    def mix(g):
        rows = pl.ds(pl.multiple_of(g * 16, 16), 16)
        mixed = dot(kron[...], xp[:, rows, :].reshape(cells, NZ))
        loc[:, rows, :] = mixed.astype(BF16).reshape(c, 16, NZ)

    pl.loop(0, 4)(mix)

    for t in reversed(range(gy - 1)):
        s = peer_y(t)
        rcopy(send2.at[t], recv2.at[s], s2s.at[t], s2r.at[s], {"gy": s}).wait_recv()
        total = total + recv2[s].astype(F32)
    sum2[...] = total

    for g in range(gx):
        send3[g, 0:18, :] = sum2[pl.ds(g, 18, stride=gx), :]

    def send_block(t):
        d = peer_x(t)
        return rcopy(send3.at[d], recv3.at[me_x], s3s.at[t], s3r.at[me_x], {"gx": d})

    for t in range(gx - 1):
        send_block(t).start()
    recv3[me_x] = send3[me_x]

    for t in range(gx - 1):
        s = peer_x(t)
        rcopy(send3.at[s], recv3.at[s], s3s.at[t], s3r.at[s], {"gx": s}).wait_recv()

    spectra = jnp.concatenate([recv3[s] for s in range(gx)], axis=1)
    sp_hi, sp_lo = split(spectra)
    mask = jnp.concatenate([mk1[...]] * gx, axis=1)
    table = None
    for p in range(2):
        rows = (dot(rep[p], sp_hi) + dot(rep[p], sp_lo)) * mask
        part = dot_split(rows, sel[p])
        table = part if table is None else table + part
    tbuf[me_s] = table

    def send_table(t):
        return rcopy(
            tbuf.at[me_s], tbuf.at[me_s], sts.at[t], str_.at[me_s], {"scene": lax.rem(me_s + t, ns)}
        )

    for t in range(1, ns):
        send_table(t).start()

    o_re, o_im = dot_split(table, orep[0]), dot_split(table, orep[1])
    grad = dot_split(w_rows[0] * o_re + w_rows[1] * o_im, selo[0])
    grad = grad + dot_split(w_rows[0] * o_im - w_rows[1] * o_re, selo[1])
    grad = grad.astype(BF16)
    mask = jnp.concatenate([mk2[...]] * (cells // 128), axis=1)
    modes = None
    for p in range(2):
        part = dot(rs[p], (dot(grad, rc[p]) * mask).astype(BF16))
        modes = part if modes is None else modes + part
    tiles = cells // 128
    send_a[...] = modes[0:16].astype(BF16)
    for p in range(2):
        for t in range(tiles):
            send_b[p * tiles + t : p * tiles + t + 1, :] = modes[16 + p : 17 + p, t * 128 : t * 128 + 128]

    def send_mode_grads(t):
        d = {"gy": peer_y(t)}
        rows = pl.ds(pl.multiple_of(me_y * 8, 8), 8)
        return (
            rcopy(send_a, recv_a.at[me_y], sas.at[t], sar.at[me_y], d),
            rcopy(send_b, recv_b.at[rows], sbs.at[t], sbr.at[me_y], d),
        )

    for t in range(gy - 1):
        for copy in send_mode_grads(t):
            copy.start()
    recv_a[me_y] = send_a[...]
    recv_b[pl.ds(pl.multiple_of(me_y * 8, 8), 8), :] = send_b[...]
    y_match = (iota((16, kx), 0)) == (iota((16, kx), 1) & 15)
    tx_now = tx[0] * phx[0, pl.ds(me_x, 1), :] - tx[1] * phx[1, pl.ds(me_x, 1), :]
    for r in range(32):
        row = jnp.where(y_match, jnp.broadcast_to(tx_now[r : r + 1], (16, kx)), 0.0)
        hi, lo = split(row)
        for q in range(gx):
            txt[q, r * 16 : r * 16 + 16, 0:128] = hi[:, q * 128 : q * 128 + 128]
            txt[q, r * 16 : r * 16 + 16, 128:256] = lo[:, q * 128 : q * 128 + 128]

    for t in range(gy - 1):
        s = peer_y(t)
        rcopy(send_a, recv_a.at[s], sas.at[t], sar.at[s], {"gy": s}).wait_recv()
        rows = pl.ds(pl.multiple_of(s * 8, 8), 8)
        rcopy(send_b, recv_b.at[rows], sbs.at[t], sbr.at[s], {"gy": s}).wait_recv()

    main = recv_a[...].reshape(16 * gy, cells)
    last = jnp.concatenate(
        [
            jnp.concatenate([recv_b[pl.ds(p * tiles + t, gy, stride=8), :] for p in range(2)], axis=0)
            for t in range(tiles)
        ],
        axis=1,
    ).astype(BF16)
    ka = 16 * gy
    back = dot(tyh[:, :ka], main) + dot(tyl[:, :ka], main)
    back = back + dot(tyh[:, ka:], last) + dot(tyl[:, ka:], last)
    send_g[...] = back.astype(BF16)

    def send_back(t):
        return rcopy(send_g, recv_g.at[me_x], sgs.at[t], sgr.at[me_x], {"gx": peer_x(t)})

    for t in range(gx - 1):
        send_back(t).start()
    recv_g[me_x] = send_g[...]

    for t in range(1, ns):
        s = lax.rem(me_s + t, ns)
        rcopy(tbuf.at[s], tbuf.at[s], sts.at[t], str_.at[s], {"scene": s}).wait_recv()
    ib = c // ns
    wide_l, wide_r = iota((128, ib * c), 1), iota((128, ib * c), 0)
    first = (wide_l >> bits) + me_s * ib
    picks = [
        one_hot(wide_r == (wide_l & (c - 1))),
        one_hot(wide_r == (wide_l & (c - 1)) + c),
        one_hot(wide_r == first + 2 * c),
        one_hot(wide_r == first + 3 * c),
    ]
    g_re = g_im = 0.0
    for s in range(ns):
        o_re, o_im, h_re, h_im = [dot_split(tbuf[s], chosen) for chosen in picks]
        g_re = g_re + o_re * h_re + o_im * h_im
        g_im = g_im + o_im * h_re - o_re * h_im
    gs_out[0] = g_re[: 9 * MZ]
    gs_out[1] = g_im[: 9 * MZ]

    pl.loop(4, 16)(mix)

    for t in range(gx - 1):
        send_planes(t).wait_send()
        send_block(t).wait_send()
    for t in range(gy - 1):
        send_modes(t).wait_send()
        for copy in send_mode_grads(t):
            copy.wait_send()
    for t in range(1, ns):
        send_table(t).wait_send()

    def back_from(s):
        gap = jnp.zeros((32, cells), BF16)
        return dot(txt[s], jnp.concatenate([recv_g[s], gap, recv_g[s], gap], axis=0))

    def arrived_back(t):
        s = peer_x(t)
        rcopy(send_g, recv_g.at[s], sgs.at[t], sgr.at[s], {"gx": s}).wait_recv()
        return back_from(s)

    b_sum[...] = back_from(me_x)

    @pl.loop(0, gx - 2)
    def _(t):
        b_sum[...] += arrived_back(t)

    b_out[...] = (b_sum[...] + arrived_back(gx - 2)).astype(BF16)
    for t in range(gx - 1):
        send_back(t).wait_send()


def final_kernel(b_ref, loc_ref, zt_ref, out_ref, zb_ref):
    block = pl.program_id(0)

    @pl.when(block == 0)
    def _():
        zb_ref[...] = jnp.zeros_like(zb_ref)
        for i in range(8):
            for p in range(2):
                zb_ref[i, p * 128 + i * 16 : p * 128 + i * 16 + 16, :] = zt_ref[p]

    lanes = pl.ds(pl.multiple_of(block * 128, 128), 128)
    lhs = jnp.concatenate([b_ref[0:256, lanes], b_ref[256:512, lanes]], axis=1)

    def finish(i, spectral):
        out_ref[i] = (spectral + loc_ref[block * 8 + i].astype(F32)).astype(BF16)

    ahead = dot(lhs, zb_ref[0])
    for i in range(8):
        now = ahead
        if i < 7:
            ahead = dot(lhs, zb_ref[i + 1])
        finish(i, now)


def body(field_in, grad_pre, spec_weight, point_weight):
    gx, gy, ns = lax.axis_size("gx"), lax.axis_size("gy"), lax.axis_size("scene")
    c = field_in.shape[1]
    cells = 16 * c
    cc = c * c
    kx = 128 * gx
    norm = float(256 * gx * gy * NZ) ** -0.5
    consts = tables(gx, gy)
    names = ["texp", "m0", "ph", "ty", "phy", "tx", "phx", "rep", "rs", "mk1", "mk2"]
    values = [jnp.asarray(consts[n]) for n in names]
    w = spec_weight.reshape(9 * MZ, 2, cc)
    inputs = [
        field_in.reshape(c, 256, NZ), grad_pre.reshape(c, 256, NZ), w, point_weight, *values
    ]
    vmem = pltpu.VMEM
    dma = pltpu.SemaphoreType.DMA
    nb = 9 * gx
    scratch = [vmem(v.shape, v.dtype) for v in inputs] + [
        vmem((112, 4 * NZ), BF16),
        vmem((gx - 1, 2, 112, NZ), BF16), vmem((gx, 2, 112, NZ), BF16),
        vmem((gy, nb, NZ), F32), vmem((gy, nb, NZ), F32),
        vmem((gy - 1, 2 * nb, 128), BF16), vmem((gy, 2 * nb, 128), BF16), vmem((2 * nb, 128), F32),
        vmem((gx, 24, 128), F32), vmem((gx, 24, 128), F32), vmem((ns, ROWS, 128), F32),
        vmem((16, cells), BF16), vmem((gy, 16, cells), BF16), vmem((8, 128), F32), vmem((8 * gy, 128), F32),
        vmem((96, cells), BF16), vmem((gx, 96, cells), BF16),
        vmem((96, 18 * gy), BF16), vmem((96, 18 * gy), BF16), vmem((gx, 512, 256), BF16), vmem((512, cells), F32),
        vmem((cells, cells), BF16),
        vmem((2, 128 * gx, 128), BF16), vmem((2, 128, cc), BF16), vmem((2, cc, 128), BF16),
        vmem((2, 128, cells), BF16), vmem((2, ROWS, cc), F32),
        dma((gx,)), dma((gx,)), dma((13,)),
        *[dma((n,)) for n in (gx, gx, gy, gy, gx, gx, gy, gy, gy, gy, gx, gx, ns, ns)],
    ]
    hbm_spec = pl.BlockSpec(memory_space=pl.ANY)
    vmem_spec = pl.BlockSpec(memory_space=pltpu.VMEM)
    b, loc, gs = pl.pallas_call(
        functools.partial(comm_kernel, gx, gy, ns, norm),
        out_shape=(
            jax.ShapeDtypeStruct((512, cells), BF16),
            jax.ShapeDtypeStruct((c, 256, NZ), BF16),
            jax.ShapeDtypeStruct((2, 9 * MZ, cc // ns), F32),
        ),
        in_specs=[hbm_spec] * len(inputs),
        out_specs=(vmem_spec, vmem_spec, vmem_spec),
        scratch_shapes=scratch,
        compiler_params=pltpu.CompilerParams(
            collective_id=0, has_side_effects=True, vmem_limit_bytes=40 * 1024 * 1024
        ),
        name="spectral_exchange",
    )(*[pltpu.with_memory_space_constraint(v, pltpu.HBM) for v in inputs])
    grad = pl.pallas_call(
        final_kernel,
        grid=(c // 8,),
        out_shape=jax.ShapeDtypeStruct((c, 256, NZ), BF16),
        in_specs=[
            vmem_spec,
            vmem_spec,
            vmem_spec,
        ],
        out_specs=pl.BlockSpec((8, 256, NZ), lambda i: (i, 0, 0)),
        scratch_shapes=[vmem((8, 256, NZ), BF16)],
        compiler_params=pltpu.CompilerParams(vmem_limit_bytes=24 * 1024 * 1024),
        name="inverse_z",
    )(b, loc, jnp.asarray(consts["zb"]))
    grad_field = grad.reshape(field_in.shape)
    grad_spec = jnp.transpose(gs, (1, 0, 2)).reshape(3, 3, MZ, 2, cc // ns)
    return grad_field, grad_spec


def solution(mesh):
    return jax.shard_map(
        body,
        mesh=mesh,
        in_specs=(
            P("scene", None, "gx", "gy", None),
            P("scene", None, "gx", "gy", None),
            P("gx", "gy", None, None, None),
            P(),
        ),
        out_specs=(P("scene", None, "gx", "gy", None), P("gx", "gy", None, None, "scene")),
        check_vma=False,
    )
```
